512 devices in a mesh: band: 32 (over z_lo, y, core), dom: 16 (over z_hi, x).
Axes of the slice: x: 4, y: 8, z: 8 (z_hi: 4, z_lo: 2; z = z_hi * 2 + z_lo), core: 2. Of those that a mesh axis runs over, the one named last changes fastest.
Arguments:
- states: float32 [4096, 8, 128, 128], P('band', None, 'dom'), may hold values from -0.015625 to 0.015625
- window: float32 [128, 8, 128, 128], P('band', None, 'dom'), may hold values from -6 to 6
- potential: float32 [8, 128, 128], P(None, 'dom'), may hold values from -3 to 3
Outputs:
- intersection: float32 [4096, 128], P('band')
- hamiltonian: float32 [4096, 128], P('band')
The draws below stay inside these ranges and needn't reach their ends.
All inputs are finite; a program needn't handle non-finite values.
Results may differ from the reference program's by a relative error of at most 0.00012.
Values sent between devices are 32-bit elements; how exact they have to be, the bound alone decides.
A program may use at most 64 MiB of HBM per device.

```python
import jax
import jax.numpy as jnp
from jax import lax

NY = 128
NZ = 8
WINDOW = 128
DEGREE = 4
NX = 128
STATES = 4096


def block_scale(own_key, extent, shards, least, high):
    factor_of, own = 1.0, jax.random.fold_in(own_key, 6)
    for axis_at, parts in shards:
        draws = jnp.exp(jax.random.uniform(jax.random.fold_in(own, axis_at), (parts,), jnp.float32, least / len(shards), high / len(shards)))
        factor_of = factor_of * jnp.repeat(draws, extent[axis_at] // parts).reshape([-1 if axis == axis_at else 1 for axis in range(len(extent))])
    return factor_of


def scatter_about(stream_key, shape, deviation, limit, pieces=(), dtype=jnp.bfloat16):
    factor_of = block_scale(stream_key, shape, pieces, -0.22, 0.18) if pieces else 1.0
    array = jax.random.normal(stream_key, shape, jnp.float32) * deviation * factor_of
    return jnp.minimum(jnp.maximum(array, -limit), limit).astype(dtype)


def setup_inputs(seed: int = 0) -> dict:
    streams_of = jax.random.split(jax.random.key(seed), 4)
    return {
        "states": scatter_about(streams_of[0], (STATES, NZ, NX, NY), (NX * NY * NZ) ** -0.5, 0.015625, ((0, 32), (2, 16)), jnp.float32),
        "window": scatter_about(streams_of[1], (WINDOW, NZ, NX, NY), 1.0, 6.0, ((0, 32), (2, 16)), jnp.float32),
        "potential": jnp.clip(jax.random.uniform(streams_of[2], (NZ, NX, NY), jnp.float32, -3.0, 3.0) * block_scale(streams_of[2], (NZ, NX, NY), ((1, 16),), -0.4, 0.0), -3.0, 3.0),
    }


coeffs = (-5369.0 / 1800.0, 12.0 / 7.0, -15.0 / 56.0, 10.0 / 189.0, -1.0 / 112.0, 2.0 / 1925.0, -1.0 / 16632.0)
centre_value = 9.0
half_width = 7.0


def apply_hamiltonian(wave_in, potential):
    z_cells = wave_in.shape[1]
    along_z = jnp.pad(wave_in, ((0, 0), (6, 6), (0, 0), (0, 0)))
    laplace = 3.0 * coeffs[0] * wave_in
    for offset in range(1, 7):
        beside = jnp.roll(wave_in, offset, 2) + jnp.roll(wave_in, -offset, 2)
        beside = beside + jnp.roll(wave_in, offset, 3) + jnp.roll(wave_in, -offset, 3)
        beside = beside + along_z[:, 6 + offset:6 + offset + z_cells] + along_z[:, 6 - offset:6 - offset + z_cells]
        laplace = laplace + coeffs[offset] * beside
    return -0.5 * laplace + potential * wave_in


def reference(states, window, potential):
    previous = window
    current = (apply_hamiltonian(window, potential) - centre_value * window) / half_width
    for repeat_index in range(DEGREE - 1):
        following = 2.0 * (apply_hamiltonian(current, potential) - centre_value * current) / half_width - previous
        previous, current = current, following
    image = apply_hamiltonian(current, potential)
    filtered = current
    states_flat = states.reshape(states.shape[0], -1)
    intersection = jnp.dot(states_flat, filtered.reshape(filtered.shape[0], -1).T, preferred_element_type=jnp.float32, precision=lax.Precision.HIGHEST)
    hamiltonian = jnp.dot(states_flat, image.reshape(image.shape[0], -1).T, preferred_element_type=jnp.float32, precision=lax.Precision.HIGHEST)
    return intersection, hamiltonian
```

```python
import jax
import jax.numpy as jnp
from jax import lax
from jax.experimental import pallas as pl
from jax.experimental.pallas import tpu as pltpu
from jax.sharding import PartitionSpec as P

COEFFS = (
    -5369.0 / 1800.0,
    12.0 / 7.0,
    -15.0 / 56.0,
    10.0 / 189.0,
    -1.0 / 112.0,
    2.0 / 1925.0,
    -1.0 / 16632.0,
)
CENTRE = 9.0
HALF_WIDTH = 7.0
MESH = pl.DeviceIdType.MESH
NY = 128
NZ = 8
TILE = 8
XN = 4
HN = 4
YN = 8
SPAN = 96
CELLS = 4096


def apply_h(source, potential, z, low, high):
    value = source[z, low:high, :]
    total = (3.0 * COEFFS[0]) * value
    for k in range(1, 7):
        beside = source[z, low + k : high + k, :] + source[z, low - k : high - k, :]
        beside = beside + pltpu.roll(value, k, 1) + pltpu.roll(value, NY - k, 1)
        if z + k < NZ:
            beside = beside + source[z + k, low:high, :]
        if z - k >= 0:
            beside = beside + source[z - k, low:high, :]
        total = total + COEFFS[k] * beside
    return -0.5 * total + potential[z, low:high, :] * value, value


def kernel(
    states, window, potential, out_f, out_h,
    even, odd, pot, image, pieces, rows, high, low, gathered, left, partial, parts, whole,
    send_w, recv_w, send_p, recv_p, local, send_s, recv_s, send_b, recv_b,
    send_up, send_down, send_z, recv_g, send_r, recv_r, send_o, recv_o,
):
    b = lax.axis_index("band")
    d = lax.axis_index("dom")
    c = lax.rem(b, 2)
    q = lax.div(b, 2)
    y = lax.rem(q, YN)
    zl = lax.div(q, YN)
    x = lax.rem(d, XN)
    h = lax.div(d, XN)

    def band_of(chip, core):
        return chip * 2 + core

    def chip_at(lo, offset):
        return lo * YN + lax.rem(y + offset + YN, YN)

    up = band_of(chip_at(zl, 1), c)
    down = band_of(chip_at(zl, -1), c)
    across = band_of((1 - zl) * YN + y, c)
    twin = band_of(q, 1 - c)

    def remote(src, dst, send, recv, band, dom):
        return pltpu.make_async_remote_copy(
            src_ref=src, dst_ref=dst, send_sem=send, recv_sem=recv,
            device_id=(band, dom), device_id_type=MESH,
        )

    barrier = pltpu.get_barrier_semaphore()

    def greet(band, dom):
        pl.semaphore_signal(barrier, inc=1, device_id=(band, dom), device_id_type=MESH)

    for k in range(1, 16):
        greet(b, lax.rem(d + k, 16))
    for k in range(16):
        greet(twin, lax.rem(d + k, 16))
    for band in (up, down, across):
        greet(band, d)
    pl.semaphore_wait(barrier, 34)

    keep = pltpu.make_async_copy(states.at[:, pl.ds(4 * c, 4)], rows.at[c], local.at[0])

    started = []

    def spread(side, column, slot_x):
        return pl.ds(pl.multiple_of(((1 - side) * XN + slot_x) * TILE, TILE), TILE)

    wide = []
    for side in (-1, 1, 0):
        row = lax.rem(h + side + HN, HN)
        for k in range(XN):
            column = lax.rem(x + k, XN)
            if side == 0 and k == 0:
                continue
            wide.append((side, row, column))
    for n, (side, row, column) in enumerate(wide):
        slot = (1 - side) * XN + x
        copy = remote(
            window.at[column], even.at[:, spread(side, column, x), :],
            send_w.at[n], recv_w.at[slot], b, row * XN + column,
        )
        copy.start()
        started.append(copy)
    for n, (side, row, column) in enumerate(wide):
        slot = (1 - side) * XN + x
        copy = remote(
            potential, pot.at[:, spread(side, column, x), :],
            send_p.at[n], recv_p.at[slot], b, row * XN + column,
        )
        copy.start()
        started.append(copy)
    own = [
        pltpu.make_async_copy(window.at[x], even.at[:, spread(0, x, x), :], local.at[1]),
        pltpu.make_async_copy(potential, pot.at[:, spread(0, x, x), :], local.at[2]),
    ]
    for copy in own:
        copy.start()
    swap = remote(
        states.at[:, pl.ds(4 * (1 - c), 4)], rows.at[c], send_s, recv_s, twin, d
    )
    swap.start()
    keep.start()
    started.append(swap)
    keep.wait()
    swap.wait_recv()

    flat_rows = rows.reshape(2 * 128 * 32, NY)

    def split_states(k, carry):
        value = flat_rows[pl.ds(k, 256, stride=32), :]
        upper = value.astype(jnp.bfloat16)
        lanes = pl.ds(pl.multiple_of(k * NY, NY), NY)
        high[:, lanes] = upper
        low[:, lanes] = (value - upper.astype(jnp.float32)).astype(jnp.bfloat16)
        return carry

    lax.fori_loop(0, 32, split_states, 0)

    for copy in own:
        copy.wait()
    for side, row, column in wide:
        slot = (1 - side) * XN + column
        spot = spread(side, column, column)
        remote(window.at[0], even.at[:, spot, :], send_w.at[0], recv_w.at[slot], b, d).wait_recv()
        remote(potential, pot.at[:, spot, :], send_p.at[0], recv_p.at[slot], b, d).wait_recv()

    for z in range(NZ):
        product, value = apply_h(even, pot, z, 8, 88)
        odd[z, 8:88, :] = (product - CENTRE * value) * (1.0 / HALF_WIDTH)
    for source, target, first, last in ((odd, even, 8, 88), (even, odd, 16, 80), (odd, even, 24, 72)):
        for z in range(NZ):
            product, value = apply_h(source, pot, z, first, last)
            target[z, first:last, :] = (
                (product - CENTRE * value) * (2.0 / HALF_WIDTH) - target[z, first:last, :]
            )

    name = c * XN + x

    def hand_on(kind, source, offset):
        for k in range(XN):
            column = lax.rem(x + k, XN)
            for j in range(2):
                core = lax.rem(c + j, 2)
                planes = pl.ds(pl.multiple_of(offset + TILE * column, TILE), TILE)
                piece = source.at[pl.ds(4 * core, 4), planes, :]
                n = (kind * XN + k) * 2 + j
                if k == 0 and j == 0:
                    copy = pltpu.make_async_copy(piece, pieces.at[name, kind], local.at[3 + kind])
                    copy.start()
                    own_pieces.append(copy)
                else:
                    copy = remote(
                        piece, pieces.at[name, kind], send_b.at[n], recv_b.at[name, kind],
                        band_of(q, core), h * XN + column,
                    )
                    copy.start()
                    started.append(copy)

    own_pieces = []
    hand_on(0, even, 32)
    for z in range(NZ):
        product, value = apply_h(even, pot, z, 32, 64)
        image[z] = product
    hand_on(1, image, 0)

    def unit(chip, kind, half):
        return gathered.at[chip, pl.ds(8 * kind, 8), pl.ds(2048 * half, 2048)]

    def forward(chip, kind, half, sems, band):
        place = unit(chip, kind, half)
        copy = remote(place, place, sems.at[chip, kind, half], recv_g.at[chip, kind, half], band, d)
        copy.start()
        started.append(copy)

    def arrive(chip, kind, half):
        place = unit(chip, kind, half)
        remote(
            place, place, send_z.at[chip, kind, half], recv_g.at[chip, kind, half], across, d
        ).wait_recv()

    flat_pieces = pieces.reshape(8 * 64, NY)

    for kind in range(2):
        own_pieces[kind].wait()
        for k in range(XN):
            for j in range(2):
                if k == 0 and j == 0:
                    continue
                source = lax.rem(c + j, 2) * XN + lax.rem(x + k, XN)
                remote(
                    image.at[pl.ds(0, 4), pl.ds(0, 8), :], pieces.at[source, kind],
                    send_b.at[0], recv_b.at[source, kind], b, d,
                ).wait_recv()
        for k in range(32):
            gathered[q, 8 * kind : 8 * kind + 8, k * NY : (k + 1) * NY] = flat_pieces[
                pl.ds(kind * 32 + k, 8, stride=64), :
            ]
        for half in range(2):
            if kind == 0:
                forward(q, 0, half, send_z, across)
            forward(q, kind, half, send_up, up)
            forward(q, kind, half, send_down, down)
            if kind == 1:
                forward(q, 1, half, send_z, across)

    other = chip_at(1 - zl, 0)
    for half in range(2):
        arrive(other, 0, half)
        forward(other, 0, half, send_up, up)
        forward(other, 0, half, send_down, down)

    def multiply(chips):
        count = 16 * len(chips)
        for n, chip in enumerate(chips):
            for k in range(8):
                lanes = slice(512 * k, 512 * (k + 1))
                value = gathered[chip, :, lanes]
                upper = value.astype(jnp.bfloat16)
                left[16 * n : 16 * n + 16, lanes] = upper
                left[count + 16 * n : count + 16 * n + 16, lanes] = (
                    value - upper.astype(jnp.float32)
                ).astype(jnp.bfloat16)
        dims = (((1,), (1,)), ((), ()))
        both = lax.dot_general(
            left[0 : 2 * count, :], high[...], dims, preferred_element_type=jnp.float32
        )
        rest = lax.dot_general(
            left[0:count, :], low[...], dims, preferred_element_type=jnp.float32
        )
        product = both[0:count] + (both[count:] + rest)
        for n, chip in enumerate(chips):
            partial[chip] = product[16 * n : 16 * n + 16]
            for core in range(2):
                copy = remote(
                    partial.at[chip, :, pl.ds(128 * core, 128)], parts.at[d * 2 + c],
                    send_r.at[chip, core], recv_r.at[d * 2 + c], band_of(q, core), chip,
                )
                away = jnp.logical_or(chip != d, c != core)
                pl.when(away)(copy.start)
                guarded.append((away, copy))

    guarded = []

    def ring_step(step):
        for kind, mine in ((0, True), (1, True), (0, False)):
            for half in range(2):
                for direction in (1, -1):
                    keeps = half == (0 if direction == 1 else 1)
                    if step == 4 and not keeps:
                        continue
                    lo = zl if mine else 1 - zl
                    chip = chip_at(lo, -direction * step)
                    arrive(chip, kind, half)
                    if step < 3 or (step == 3 and keeps):
                        if direction == 1:
                            forward(chip, kind, half, send_up, up)
                        else:
                            forward(chip, kind, half, send_down, down)
                    if kind == 1:
                        forward(chip, kind, half, send_z, across)

    def cross(offset):
        for half in range(2):
            arrive(chip_at(1 - zl, offset), 1, half)

    ring_step(1)
    cross(0)
    multiply([q, other])
    for step in range(2, 5):
        ring_step(step)
        cross(step - 1)
        cross(1 - step)
        multiply([chip_at(lo, o) for lo in (zl, 1 - zl) for o in (step - 1, 1 - step)])
    cross(4)
    multiply([chip_at(zl, 4), chip_at(1 - zl, 4)])

    for j in range(2):
        for k in range(16):
            if j == 0 and k == 0:
                continue
            source = lax.rem(d + k, 16) * 2 + lax.rem(c + j, 2)
            remote(
                partial.at[0, :, pl.ds(0, 128)], parts.at[source],
                send_r.at[0, 0], recv_r.at[source], b, d,
            ).wait_recv()
    total = partial[d, :, pl.ds(pl.multiple_of(128 * c, 128), 128)]
    for j in range(2):
        for k in range(16):
            if j == 0 and k == 0:
                continue
            total = total + parts[lax.rem(d + k, 16) * 2 + lax.rem(c + j, 2)]
    whole[d] = total
    for k in range(1, 16):
        copy = remote(
            whole.at[d], whole.at[d], send_o.at[k], recv_o.at[d], b, lax.rem(d + k, 16)
        )
        copy.start()
        started.append(copy)
    for k in range(1, 16):
        source = lax.rem(d + k, 16)
        remote(
            whole.at[source], whole.at[source], send_o.at[k], recv_o.at[source], b, d
        ).wait_recv()
    out_f[...] = whole[:, 0:8, :].reshape(128, 128).T
    out_h[...] = whole[:, 8:16, :].reshape(128, 128).T

    for copy in started:
        copy.wait_send()
    for away, copy in guarded:
        pl.when(away)(copy.wait_send)


def per_device(states, window, potential):
    f32 = jnp.float32
    dma = pltpu.SemaphoreType.DMA
    vmem = pltpu.VMEM
    return pl.pallas_call(
        kernel,
        out_shape=(
            jax.ShapeDtypeStruct((128, 128), f32),
            jax.ShapeDtypeStruct((128, 128), f32),
        ),
        in_specs=[pl.BlockSpec(memory_space=pl.ANY)] * 3,
        out_specs=(pl.BlockSpec(memory_space=pltpu.VMEM),) * 2,
        scratch_shapes=[
            vmem((NZ, SPAN, NY), f32),
            vmem((NZ, SPAN, NY), f32),
            vmem((NZ, SPAN, NY), f32),
            vmem((NZ, 32, NY), f32),
            vmem((8, 2, 4, TILE, NY), f32),
            vmem((2, 128, 4, TILE, NY), f32),
            vmem((256, CELLS), jnp.bfloat16),
            vmem((256, CELLS), jnp.bfloat16),
            vmem((16, 16, CELLS), f32),
            vmem((128, CELLS), jnp.bfloat16),
            vmem((16, 16, 256), f32),
            vmem((32, 16, 128), f32),
            vmem((16, 16, 128), f32),
            dma((12,)), dma((12,)), dma((12,)), dma((12,)),
            dma((5,)), dma, dma,
            dma((16,)), dma((8, 2)),
            dma((16, 2, 2)), dma((16, 2, 2)), dma((16, 2, 2)), dma((16, 2, 2)),
            dma((16, 2)), dma((32,)), dma((16,)), dma((16,)),
        ],
        compiler_params=pltpu.CompilerParams(
            collective_id=0, has_side_effects=True, vmem_limit_bytes=60 * 1024 * 1024
        ),
    )(states, window, potential)


def solution(mesh):
    in_specs = (P("band", None, "dom", None), P("band", None, "dom", None), P(None, "dom", None))
    out_specs = (P("band", None), P("band", None))
    return jax.shard_map(
        per_device, mesh=mesh, in_specs=in_specs, out_specs=out_specs, check_vma=False
    )
```

```python
import jax
import jax.numpy as jnp
from jax import lax
from jax.experimental import pallas as pl
from jax.experimental.pallas import tpu as pltpu
from jax.sharding import PartitionSpec as P

COEFFS = (
    -5369.0 / 1800.0,
    12.0 / 7.0,
    -15.0 / 56.0,
    10.0 / 189.0,
    -1.0 / 112.0,
    2.0 / 1925.0,
    -1.0 / 16632.0,
)
CENTRE = 9.0
HALF_WIDTH = 7.0
MESH = pl.DeviceIdType.MESH
NY = 128
NZ = 8
TILE = 8
XN = 4
HN = 4
YN = 8
SPAN = 96
CELLS = 4096


def apply_h(source, potential, z, low, high):
    value = source[z, low:high, :]
    total = (3.0 * COEFFS[0]) * value
    for k in range(1, 7):
        beside = source[z, low + k : high + k, :] + source[z, low - k : high - k, :]
        beside = beside + pltpu.roll(value, k, 1) + pltpu.roll(value, NY - k, 1)
        if z + k < NZ:
            beside = beside + source[z + k, low:high, :]
        if z - k >= 0:
            beside = beside + source[z - k, low:high, :]
        total = total + COEFFS[k] * beside
    return -0.5 * total + potential[z, low:high, :] * value, value


def kernel(
    states, window, potential, out,
    even, odd, pot, image, rows, high, low, gathered, left, partial, parts, whole,
    send_w, recv_w, send_p, recv_p, send_t, recv_t, local, send_s, recv_s, send_b, recv_b,
    send_up, send_down, send_z, recv_g, send_r, recv_r, send_o, recv_o,
):
    b = lax.axis_index("band")
    d = lax.axis_index("dom")
    c = lax.rem(b, 2)
    q = lax.div(b, 2)
    y = lax.rem(q, YN)
    zl = lax.div(q, YN)
    x = lax.rem(d, XN)
    h = lax.div(d, XN)

    def band_of(chip, core):
        return chip * 2 + core

    def chip_at(lo, offset):
        return lo * YN + lax.rem(y + offset + YN, YN)

    up = band_of(chip_at(zl, 1), c)
    down = band_of(chip_at(zl, -1), c)
    across = band_of((1 - zl) * YN + y, c)
    twin = band_of(q, 1 - c)
    columns = [lax.rem(x + k, XN) for k in range(XN)]

    def remote(src, dst, send, recv, band, dom):
        return pltpu.make_async_remote_copy(
            src_ref=src, dst_ref=dst, send_sem=send, recv_sem=recv,
            device_id=(band, dom), device_id_type=MESH,
        )

    wide = []
    for side in (-1, 1, 0):
        row = lax.rem(h + side + HN, HN)
        for k in range(XN):
            if side != 0 or k != 0:
                wide.append((side, row, columns[k]))
    barrier = pltpu.get_barrier_semaphore()

    def greet(band, dom):
        pl.semaphore_signal(barrier, inc=1, device_id=(band, dom), device_id_type=MESH)

    for side, row, column in wide:
        greet(b, row * XN + column)
    for k in range(XN):
        greet(twin, h * XN + columns[k])
    for band in (up, down, across):
        greet(band, d)
    pl.semaphore_wait(barrier, 18)

    started = []

    def begin(copy):
        copy.start()
        started.append(copy)

    def planes(side, slot_x):
        return pl.ds(pl.multiple_of(((1 - side) * XN + slot_x) * TILE, TILE), TILE)

    mine = pl.ds(4 * c, 4)

    def met(side, column):
        if side == 1:
            return column != 0
        return column != XN - 1

    guarded = []
    for n, (side, row, column) in enumerate(wide):
        copy = remote(
            potential.at[mine], pot.at[mine, planes(side, x), :],
            send_p.at[n], recv_p.at[(1 - side) * XN + x], b, row * XN + column,
        )
        if side == 0:
            begin(copy)
        else:
            sent = met(side, x)
            pl.when(sent)(copy.start)
            guarded.append((sent, copy))
    for n, (side, row, column) in enumerate(wide):
        begin(
            remote(
                window.at[column], even.at[:, planes(side, x), :],
                send_w.at[n], recv_w.at[(1 - side) * XN + x], b, row * XN + column,
            )
        )
    own = [
        pltpu.make_async_copy(window.at[x], even.at[:, planes(0, x), :], local.at[1]),
        pltpu.make_async_copy(potential.at[mine], pot.at[mine, planes(0, x), :], local.at[2]),
    ]
    for copy in own:
        copy.start()
    keep = pltpu.make_async_copy(states.at[:, mine], rows.at[c], local.at[0])
    keep.start()
    swap = remote(states.at[:, pl.ds(4 * (1 - c), 4)], rows.at[c], send_s, recv_s, twin, d)
    begin(swap)

    flat_rows = rows.reshape(2 * 128 * 32, NY)

    def split_states(core):
        def body(k, carry):
            value = flat_rows[pl.ds(core * 4096 + k, 128, stride=32), :].T
            upper = value.astype(jnp.bfloat16)
            cells = pl.ds(pl.multiple_of(k * NY, NY), NY)
            lanes = pl.ds(pl.multiple_of(core * 128, 128), 128)
            high[cells, lanes] = upper
            low[cells, lanes] = (value - upper.astype(jnp.float32)).astype(jnp.bfloat16)
            return carry

        lax.fori_loop(0, 32, body, 0)

    keep.wait()
    split_states(c)

    own[1].wait()
    for n, side in enumerate((-1, 1, 0)):
        for place, row, column in wide:
            if place != side:
                continue
            copy = remote(
                potential.at[mine], pot.at[mine, planes(side, column), :],
                send_p.at[0], recv_p.at[(1 - side) * XN + column], b, d,
            )
            if side == 0:
                copy.wait_recv()
            else:
                pl.when(met(side, column))(copy.wait_recv)
        low_row, high_row = {1: (8, 32), 0: (32, 64), -1: (64, 88)}[side]
        strip = pot.at[mine, pl.ds(low_row, high_row - low_row), :]
        begin(remote(strip, strip, send_t.at[n], recv_t.at[n], twin, d))

    own[0].wait()
    for side, row, column in wide:
        remote(
            window.at[0], even.at[:, planes(side, column), :],
            send_w.at[0], recv_w.at[(1 - side) * XN + column], b, d,
        ).wait_recv()
    for n, side in enumerate((-1, 1, 0)):
        low_row, high_row = {1: (8, 32), 0: (32, 64), -1: (64, 88)}[side]
        strip = pot.at[pl.ds(4 * (1 - c), 4), pl.ds(low_row, high_row - low_row), :]
        remote(strip, strip, send_t.at[n], recv_t.at[n], twin, d).wait_recv()

    for z in range(NZ):
        product, value = apply_h(even, pot, z, 8, 88)
        odd[z, 8:88, :] = (product - CENTRE * value) * (1.0 / HALF_WIDTH)
    for source, target, first, last in ((odd, even, 8, 88), (even, odd, 16, 80), (odd, even, 24, 72)):
        for z in range(NZ):
            product, value = apply_h(source, pot, z, first, last)
            target[z, first:last, :] = (
                (product - CENTRE * value) * (2.0 / HALF_WIDTH) - target[z, first:last, :]
            )

    own_pieces = []

    def hand_on(kind, source, offset):
        for k in (0, 2, 1, 3):
            for j in range(2):
                core = lax.rem(c + j, 2)
                place = pl.ds(pl.multiple_of(offset + TILE * columns[k], TILE), TILE)
                piece = source.at[pl.ds(4 * core, 4), place, :]
                goal = gathered.at[q, kind, x, c]
                if k == 0 and j == 0:
                    copy = pltpu.make_async_copy(piece, goal, local.at[3 + kind])
                    copy.start()
                    own_pieces.append(copy)
                else:
                    begin(
                        remote(
                            piece, goal, send_b.at[kind, k, j], recv_b.at[kind, x, c],
                            band_of(q, core), h * XN + columns[k],
                        )
                    )

    hand_on(0, even, 32)
    for z in range(NZ):
        product, value = apply_h(even, pot, z, 32, 64)
        image[z] = product
    hand_on(1, image, 0)

    def forward(chip, kind, k, sems, band):
        place = gathered.at[chip, kind, columns[k]]
        begin(
            remote(place, place, sems.at[chip, kind, k], recv_g.at[chip, kind, k], band, d)
        )

    def arrive(chip, kind, k):
        place = gathered.at[chip, kind, columns[k]]
        remote(
            place, place, send_z.at[chip, kind, k], recv_g.at[chip, kind, k], across, d
        ).wait_recv()

    order = ((0, 0), (0, 1), (0, 3), (1, 0), (0, 2), (1, 1), (1, 3), (1, 2))
    for kind, k in order:
        for j in range(2):
            if k == 0 and j == 0:
                own_pieces[kind].wait()
                continue
            core = lax.rem(c + j, 2)
            remote(
                image.at[pl.ds(0, 4), pl.ds(0, TILE), :], gathered.at[q, kind, columns[k], core],
                send_b.at[0, 0, 0], recv_b.at[kind, columns[k], core], b, d,
            ).wait_recv()
        if kind == 0:
            forward(q, 0, k, send_z, across)
        forward(q, kind, k, send_up, up)
        forward(q, kind, k, send_down, down)
        if kind == 1:
            forward(q, 1, k, send_z, across)

    other = chip_at(1 - zl, 0)
    for k in (0, 1, 3, 2):
        arrive(other, 0, k)
        forward(other, 0, k, send_up, up)
        forward(other, 0, k, send_down, down)

    swap.wait_recv()
    split_states(1 - c)

    flat_pieces = gathered.reshape(16 * 512, NY)

    def multiply(chips):
        count = 16 * len(chips)
        for n, chip in enumerate(chips):
            for k in range(32):
                lanes = slice(NY * k, NY * (k + 1))
                value = flat_pieces[pl.ds(chip * 512 + k, 16, stride=32), :]
                upper = value.astype(jnp.bfloat16)
                left[16 * n : 16 * n + 16, lanes] = upper
                left[count + 16 * n : count + 16 * n + 16, lanes] = (
                    value - upper.astype(jnp.float32)
                ).astype(jnp.bfloat16)
        both = jnp.dot(left[0 : 2 * count, :], high[...], preferred_element_type=jnp.float32)
        rest = jnp.dot(left[0:count, :], low[...], preferred_element_type=jnp.float32)
        product = both[0:count] + (both[count:] + rest)
        for n, chip in enumerate(chips):
            partial[chip] = product[16 * n : 16 * n + 16]
            for core in range(2):
                copy = remote(
                    partial.at[chip, :, pl.ds(128 * core, 128)], parts.at[d * 2 + c],
                    send_r.at[chip, core], recv_r.at[d * 2 + c], band_of(q, core), chip,
                )
                away = jnp.logical_or(chip != d, c != core)
                pl.when(away)(copy.start)
                guarded.append((away, copy))

    def reduce_own():
        def take(source, total):
            remote(
                partial.at[0, :, pl.ds(0, 128)], parts.at[source],
                send_r.at[0, 0], recv_r.at[source], b, d,
            ).wait_recv()
            return total + parts[source]

        total = partial[d, :, pl.ds(pl.multiple_of(128 * c, 128), 128)]
        total = lax.fori_loop(
            0, 16, lambda k, t: take(lax.rem(d + k, 16) * 2 + (1 - c), t), total
        )
        total = lax.fori_loop(1, 16, lambda k, t: take(lax.rem(d + k, 16) * 2 + c, t), total)
        whole[d] = total
        for k in range(1, 16):
            remote(
                whole.at[d], whole.at[d], send_o.at[k], recv_o.at[d], b, lax.rem(d + k, 16)
            ).start()

    ahead = lax.rem(lax.rem(d, YN) - y + YN, YN)
    turn = jnp.minimum(ahead, YN - ahead) + jnp.where(lax.div(d, YN) == zl, 0, 1)

    def ring_step(step):
        units = [(zl, kind, k) for kind, k in order] + [(1 - zl, 0, k) for k in (0, 1, 3, 2)]
        for lo, kind, k in units:
            for direction in (1, -1):
                keeps = (k < 2) == (direction == 1)
                if step == 4 and not keeps:
                    continue
                chip = chip_at(lo, -direction * step)
                arrive(chip, kind, k)
                if step < 3 or (step == 3 and keeps):
                    if direction == 1:
                        forward(chip, kind, k, send_up, up)
                    else:
                        forward(chip, kind, k, send_down, down)
                if kind == 1:
                    forward(chip, kind, k, send_z, across)

    def cross(offset):
        for k in (0, 1, 3, 2):
            arrive(chip_at(1 - zl, offset), 1, k)

    multiply([q])
    for step in range(1, 5):
        ring_step(step)
        behind = [0] if step == 1 else [step - 1, 1 - step]
        for offset in behind:
            cross(offset)
        level = [4] if step == 4 else [step, -step]
        multiply([chip_at(zl, o) for o in level] + [chip_at(1 - zl, o) for o in behind])
        pl.when(turn == step - 1)(reduce_own)
    cross(4)
    multiply([chip_at(1 - zl, 4)])
    pl.when(turn >= 4)(reduce_own)
    for k in range(1, 16):
        source = lax.rem(d + k, 16)
        remote(
            whole.at[source], whole.at[source], send_o.at[k], recv_o.at[source], b, d
        ).wait_recv()
    out[...] = whole[...]

    for copy in started:
        copy.wait_send()
    for sent, copy in guarded:
        pl.when(sent)(copy.wait_send)
    for k in range(1, 16):
        remote(
            whole.at[d], whole.at[d], send_o.at[k], recv_o.at[d], b, lax.rem(d + k, 16)
        ).wait_send()


def finish(whole, out_f, out_h, turned):
    flat = whole.reshape(256, 128)
    for kind, out in ((0, out_f), (1, out_h)):
        for column in range(XN):
            for core in range(2):
                turned[pl.ds(4 * core + column, 16, stride=8), :] = flat[
                    pl.ds(8 * kind + 2 * column + core, 16, stride=16), :
                ]
        out[...] = turned[...].T


def per_device(states, window, potential):
    f32 = jnp.float32
    dma = pltpu.SemaphoreType.DMA
    vmem = pltpu.VMEM
    whole = pl.pallas_call(
        kernel,
        out_shape=jax.ShapeDtypeStruct((16, 16, 128), f32),
        in_specs=[pl.BlockSpec(memory_space=pl.ANY)] * 3,
        out_specs=pl.BlockSpec(memory_space=pltpu.VMEM),
        scratch_shapes=[
            vmem((NZ, SPAN, NY), f32),
            vmem((NZ, SPAN, NY), f32),
            vmem((NZ, SPAN, NY), f32),
            vmem((NZ, 32, NY), f32),
            vmem((2, 128, 4, TILE, NY), f32),
            vmem((CELLS, 256), jnp.bfloat16),
            vmem((CELLS, 256), jnp.bfloat16),
            vmem((16, 2, XN, 2, 4, TILE, NY), f32),
            vmem((128, CELLS), jnp.bfloat16),
            vmem((16, 16, 256), f32),
            vmem((32, 16, 128), f32),
            vmem((16, 16, 128), f32),
            dma((12,)), dma((12,)), dma((12,)), dma((12,)), dma((3,)), dma((3,)),
            dma((5,)), dma, dma,
            dma((2, XN, 2)), dma((2, XN, 2)),
            dma((16, 2, XN)), dma((16, 2, XN)), dma((16, 2, XN)), dma((16, 2, XN)),
            dma((16, 2)), dma((32,)), dma((16,)), dma((16,)),
        ],
        compiler_params=pltpu.CompilerParams(
            collective_id=0, has_side_effects=True, vmem_limit_bytes=60 * 1024 * 1024
        ),
    )(states, window, potential)
    return pl.pallas_call(
        finish,
        out_shape=(
            jax.ShapeDtypeStruct((128, 128), f32),
            jax.ShapeDtypeStruct((128, 128), f32),
        ),
        in_specs=[pl.BlockSpec(memory_space=pltpu.VMEM)],
        out_specs=(pl.BlockSpec(memory_space=pltpu.VMEM),) * 2,
        scratch_shapes=[vmem((128, 128), f32)],
    )(whole)


def solution(mesh):
    in_specs = (P("band", None, "dom", None), P("band", None, "dom", None), P(None, "dom", None))
    out_specs = (P("band", None), P("band", None))
    return jax.shard_map(
        per_device, mesh=mesh, in_specs=in_specs, out_specs=out_specs, check_vma=False
    )
```

```python
import jax
import jax.numpy as jnp
from jax import lax
from jax.experimental import pallas as pl
from jax.experimental.pallas import tpu as pltpu
from jax.sharding import PartitionSpec as P

COEFFS = (
    -5369.0 / 1800.0,
    12.0 / 7.0,
    -15.0 / 56.0,
    10.0 / 189.0,
    -1.0 / 112.0,
    2.0 / 1925.0,
    -1.0 / 16632.0,
)
CENTRE = 9.0
HALF_WIDTH = 7.0
MESH = pl.DeviceIdType.MESH
NY = 128
NZ = 8
TILE = 8
XN = 4
HN = 4
YN = 8
SPAN = 96
CELLS = 4096


def apply_h(source, potential, z, low, high):
    value = source[z, low:high, :]
    total = (3.0 * COEFFS[0]) * value
    for k in range(1, 7):
        beside = source[z, low + k : high + k, :] + source[z, low - k : high - k, :]
        beside = beside + pltpu.roll(value, k, 1) + pltpu.roll(value, NY - k, 1)
        if z + k < NZ:
            beside = beside + source[z + k, low:high, :]
        if z - k >= 0:
            beside = beside + source[z - k, low:high, :]
        total = total + COEFFS[k] * beside
    if potential is None:
        return -0.5 * total, value
    return -0.5 * total + potential[z, low:high, :] * value, value


def kernel(
    states, window, potential, out,
    even, odd, pot, image, rows, high, low, gathered, left, partial, parts, whole, near, far,
    send_w, recv_w, send_p, recv_p, send_t, recv_t, local, send_s, recv_s, send_b, recv_b,
    send_up, send_down, send_z, recv_g, send_r, recv_r, send_o, recv_o,
    send_near, recv_near, send_far, recv_far,
):
    b = lax.axis_index("band")
    d = lax.axis_index("dom")
    c = lax.rem(b, 2)
    q = lax.div(b, 2)
    y = lax.rem(q, YN)
    zl = lax.div(q, YN)
    x = lax.rem(d, XN)
    h = lax.div(d, XN)

    def band_of(chip, core):
        return chip * 2 + core

    def chip_at(lo, offset):
        return lo * YN + lax.rem(y + offset + YN, YN)

    up = band_of(chip_at(zl, 1), c)
    down = band_of(chip_at(zl, -1), c)
    across = band_of((1 - zl) * YN + y, c)
    twin = band_of(q, 1 - c)
    columns = [lax.rem(x + k, XN) for k in range(XN)]

    def remote(src, dst, send, recv, band, dom):
        return pltpu.make_async_remote_copy(
            src_ref=src, dst_ref=dst, send_sem=send, recv_sem=recv,
            device_id=(band, dom), device_id_type=MESH,
        )

    wide = []
    for side in (-1, 1, 0):
        row = lax.rem(h + side + HN, HN)
        for k in range(XN):
            if side != 0 or k != 0:
                wide.append((side, row, columns[k]))
    barrier = pltpu.get_barrier_semaphore()

    def greet(band, dom):
        pl.semaphore_signal(barrier, inc=1, device_id=(band, dom), device_id_type=MESH)

    for side, row, column in wide:
        greet(b, row * XN + column)
    for k in range(XN):
        greet(twin, h * XN + columns[k])
    for band in (up, down, across):
        greet(band, d)
    pl.semaphore_wait(barrier, 18)

    started = []

    def begin(copy):
        copy.start()
        started.append(copy)

    def planes(side, slot_x):
        return pl.ds(pl.multiple_of(((1 - side) * XN + slot_x) * TILE, TILE), TILE)

    mine = pl.ds(4 * c, 4)

    def met(side, column):
        if side == 1:
            return column != 0
        return column != XN - 1

    guarded = []
    for n, (side, row, column) in enumerate(wide):
        copy = remote(
            potential.at[mine], pot.at[mine, planes(side, x), :],
            send_p.at[n], recv_p.at[(1 - side) * XN + x], b, row * XN + column,
        )
        if side == 0:
            begin(copy)
        else:
            sent = met(side, x)
            pl.when(sent)(copy.start)
            guarded.append((sent, copy))
    for n, (side, row, column) in enumerate(wide):
        begin(
            remote(
                window.at[column], even.at[:, planes(side, x), :],
                send_w.at[n], recv_w.at[(1 - side) * XN + x], b, row * XN + column,
            )
        )
    own = [
        pltpu.make_async_copy(window.at[x], even.at[:, planes(0, x), :], local.at[1]),
        pltpu.make_async_copy(potential.at[mine], pot.at[mine, planes(0, x), :], local.at[2]),
    ]
    for copy in own:
        copy.start()
    keep = pltpu.make_async_copy(states.at[:, mine], rows.at[c], local.at[0])
    keep.start()
    swap = remote(states.at[:, pl.ds(4 * (1 - c), 4)], rows.at[c], send_s, recv_s, twin, d)
    begin(swap)

    flat_rows = rows.reshape(2 * 128 * 32, NY)

    def split_states(core):
        def body(turn, carry):
            for n in range(4):
                k = 4 * turn + n
                value = flat_rows[pl.ds(core * 4096 + k, 128, stride=32), :].T
                upper = value.astype(jnp.bfloat16)
                cells = pl.ds(pl.multiple_of(k * NY, NY), NY)
                lanes = pl.ds(pl.multiple_of(core * 128, 128), 128)
                high[cells, lanes] = upper
                low[cells, lanes] = (value - upper.astype(jnp.float32)).astype(jnp.bfloat16)
            return carry

        lax.fori_loop(0, 8, body, 0)

    keep.wait()
    split_states(c)
    swap.wait_recv()
    split_states(1 - c)

    own[1].wait()
    for n, side in enumerate((-1, 1, 0)):
        for place, row, column in wide:
            if place != side:
                continue
            copy = remote(
                potential.at[mine], pot.at[mine, planes(side, column), :],
                send_p.at[0], recv_p.at[(1 - side) * XN + column], b, d,
            )
            if side == 0:
                copy.wait_recv()
            else:
                pl.when(met(side, column))(copy.wait_recv)
        low_row, high_row = {1: (8, 32), 0: (32, 64), -1: (64, 88)}[side]
        strip = pot.at[mine, pl.ds(low_row, high_row - low_row), :]
        begin(remote(strip, strip, send_t.at[n], recv_t.at[n], twin, d))

    own[0].wait()
    for side, row, column in wide:
        remote(
            window.at[0], even.at[:, planes(side, column), :],
            send_w.at[0], recv_w.at[(1 - side) * XN + column], b, d,
        ).wait_recv()

    for z in range(NZ):
        product, value = apply_h(even, None, z, 8, 88)
        odd[z, 8:88, :] = (product - CENTRE * value) * (1.0 / HALF_WIDTH)
    for n, side in enumerate((-1, 1, 0)):
        low_row, high_row = {1: (8, 32), 0: (32, 64), -1: (64, 88)}[side]
        strip = pot.at[pl.ds(4 * (1 - c), 4), pl.ds(low_row, high_row - low_row), :]
        remote(strip, strip, send_t.at[n], recv_t.at[n], twin, d).wait_recv()
    for z in range(NZ):
        odd[z, 8:88, :] += pot[z, 8:88, :] * even[z, 8:88, :] * (1.0 / HALF_WIDTH)
    for source, target, first, last in ((odd, even, 8, 88), (even, odd, 16, 80), (odd, even, 24, 72)):
        for z in range(NZ):
            product, value = apply_h(source, pot, z, first, last)
            target[z, first:last, :] = (
                (product - CENTRE * value) * (2.0 / HALF_WIDTH) - target[z, first:last, :]
            )

    own_pieces = []

    def hand_on(kind, source, offset):
        for k in (0, 2, 1, 3):
            for j in range(2):
                core = lax.rem(c + j, 2)
                place = pl.ds(pl.multiple_of(offset + TILE * columns[k], TILE), TILE)
                piece = source.at[pl.ds(4 * core, 4), place, :]
                goal = gathered.at[q, kind, x, c]
                if k == 0 and j == 0:
                    copy = pltpu.make_async_copy(piece, goal, local.at[3 + kind])
                    copy.start()
                    own_pieces.append(copy)
                else:
                    begin(
                        remote(
                            piece, goal, send_b.at[kind, k, j], recv_b.at[kind, x, c],
                            band_of(q, core), h * XN + columns[k],
                        )
                    )

    hand_on(0, even, 32)
    for z in range(NZ):
        product, value = apply_h(even, pot, z, 32, 64)
        image[z] = product
    hand_on(1, image, 0)

    def forward(chip, kind, k, sems, band):
        place = gathered.at[chip, kind, columns[k]]
        begin(
            remote(place, place, sems.at[chip, kind, k], recv_g.at[chip, kind, k], band, d)
        )

    def arrive(chip, kind, k):
        place = gathered.at[chip, kind, columns[k]]
        remote(
            place, place, send_z.at[chip, kind, k], recv_g.at[chip, kind, k], across, d
        ).wait_recv()

    order = ((0, 0), (0, 1), (0, 3), (1, 0), (0, 2), (1, 1), (1, 3), (1, 2))
    for kind, k in order:
        for j in range(2):
            if k == 0 and j == 0:
                own_pieces[kind].wait()
                continue
            core = lax.rem(c + j, 2)
            remote(
                image.at[pl.ds(0, 4), pl.ds(0, TILE), :], gathered.at[q, kind, columns[k], core],
                send_b.at[0, 0, 0], recv_b.at[kind, columns[k], core], b, d,
            ).wait_recv()
        if kind == 0:
            forward(q, 0, k, send_z, across)
        forward(q, kind, k, send_up, up)
        forward(q, kind, k, send_down, down)
        if kind == 1:
            forward(q, 1, k, send_z, across)

    other = chip_at(1 - zl, 0)
    for k in (0, 1, 3, 2):
        arrive(other, 0, k)
        forward(other, 0, k, send_up, up)
        forward(other, 0, k, send_down, down)

    flat_pieces = gathered.reshape(16 * 512, NY)

    def multiply(chips, last=False):
        count = 16 * len(chips)
        for n, chip in enumerate(chips):
            for k in range(32):
                lanes = slice(NY * k, NY * (k + 1))
                value = flat_pieces[pl.ds(chip * 512 + k, 16, stride=32), :]
                upper = value.astype(jnp.bfloat16)
                left[16 * n : 16 * n + 16, lanes] = upper
                left[count + 16 * n : count + 16 * n + 16, lanes] = (
                    value - upper.astype(jnp.float32)
                ).astype(jnp.bfloat16)
        both = jnp.dot(left[0 : 2 * count, :], high[...], preferred_element_type=jnp.float32)
        rest = jnp.dot(left[0:count, :], low[...], preferred_element_type=jnp.float32)
        product = both[0:count] + (both[count:] + rest)
        for n, chip in enumerate(chips):
            partial[chip] = product[16 * n : 16 * n + 16]
            if last:
                continue
            for core in range(2):
                copy = remote(
                    partial.at[chip, :, pl.ds(128 * core, 128)], parts.at[d * 2 + c],
                    send_r.at[chip, core], recv_r.at[d * 2 + c], band_of(q, core), chip,
                )
                away = jnp.logical_or(chip != d, c != core)
                pl.when(away)(copy.start)
                guarded.append((away, copy))

    def reduce_own():
        def take(source, total):
            remote(
                partial.at[0, :, pl.ds(0, 128)], parts.at[source],
                send_r.at[0, 0], recv_r.at[source], b, d,
            ).wait_recv()
            return total + parts[source]

        total = partial[d, :, pl.ds(pl.multiple_of(128 * c, 128), 128)]
        total = lax.fori_loop(
            0, 16, lambda k, t: take(lax.rem(d + k, 16) * 2 + (1 - c), t), total
        )
        total = lax.fori_loop(1, 16, lambda k, t: take(lax.rem(d + k, 16) * 2 + c, t), total)
        whole[d] = total
        for k in range(1, 16):
            remote(
                whole.at[d], whole.at[d], send_o.at[k], recv_o.at[d], b, lax.rem(d + k, 16)
            ).start()

    ahead = lax.rem(lax.rem(d, YN) - y + YN, YN)
    turn = jnp.minimum(ahead, YN - ahead) + jnp.where(lax.div(d, YN) == zl, 0, 1)

    def ring_step(step):
        units = [(lo, kind, k) for lo, kind in ((zl, 1), (zl, 0), (1 - zl, 0)) for k in (0, 1, 3, 2)]
        for lo, kind, k in units:
            for direction in (1, -1):
                keeps = (k < 2) == (direction == 1)
                if step == 4 and not keeps:
                    continue
                chip = chip_at(lo, -direction * step)
                arrive(chip, kind, k)
                if step < 3 or (step == 3 and keeps):
                    if direction == 1:
                        forward(chip, kind, k, send_up, up)
                    else:
                        forward(chip, kind, k, send_down, down)
                if kind == 1:
                    forward(chip, kind, k, send_z, across)

    def cross(offset):
        for k in (0, 1, 3, 2):
            arrive(chip_at(1 - zl, offset), 1, k)

    for step in range(1, 5):
        ring_step(step)
        behind = [0] if step == 1 else [step - 1, 1 - step]
        for offset in behind:
            cross(offset)
        level = {1: [0, 1, -1], 4: [4]}.get(step, [step, -step])
        multiply([chip_at(zl, o) for o in level] + [chip_at(1 - zl, o) for o in behind])
        if step == 2:
            pl.when(turn <= 1)(reduce_own)
        if step == 3:
            pl.when(turn == 2)(reduce_own)
    cross(4)
    final = chip_at(1 - zl, 4)
    multiply([final], last=True)
    for k in (2, 1, 3, 0):
        for j in range(2):
            core = lax.rem(c + j, 2)
            part = partial.at[final, :, pl.ds(pl.multiple_of(128 * core, 128), 128)]
            if k == 0 and j == 0:
                near[x, c] = part[...]
            else:
                begin(
                    remote(
                        part, near.at[x, c], send_near.at[k, j], recv_near.at[x, c],
                        band_of(q, core), h * XN + columns[k],
                    )
                )
    pl.when(jnp.logical_or(turn == 3, turn == 4))(reduce_own)
    for k in range(XN):
        for j in range(2):
            if k != 0 or j != 0:
                core = lax.rem(c + j, 2)
                remote(
                    near.at[x, c], near.at[columns[k], core], send_near.at[0, 1],
                    recv_near.at[columns[k], core], b, d,
                ).wait_recv()
    total = near[0, 0] + near[0, 1]
    for column in range(1, XN):
        total = total + (near[column, 0] + near[column, 1])
    far[h] = total
    for k in (2, 1, 3):
        begin(
            remote(
                far.at[h], far.at[h], send_far.at[k], recv_far.at[h],
                b, lax.rem(h + k, HN) * XN + x,
            )
        )
    for k in range(1, 16):
        source = lax.rem(d + k, 16)
        copy = remote(whole.at[source], whole.at[source], send_o.at[k], recv_o.at[source], b, d)
        pl.when(source != final)(copy.wait_recv)
    for k in range(1, HN):
        row = lax.rem(h + k, HN)
        remote(far.at[h], far.at[row], send_far.at[k], recv_far.at[row], b, d).wait_recv()
    whole[final] = (far[0] + far[1]) + (far[2] + far[3])
    out[...] = whole[...]

    for copy in started:
        copy.wait_send()
    for sent, copy in guarded:
        pl.when(sent)(copy.wait_send)
    for k in range(1, 16):
        copy = remote(whole.at[d], whole.at[d], send_o.at[k], recv_o.at[d], b, lax.rem(d + k, 16))
        pl.when(d != final)(copy.wait_send)


def finish(whole, out_f, out_h, turned):
    flat = whole.reshape(256, 128)
    for kind, out in ((0, out_f), (1, out_h)):
        for column in range(XN):
            for core in range(2):
                turned[pl.ds(4 * core + column, 16, stride=8), :] = flat[
                    pl.ds(8 * kind + 2 * column + core, 16, stride=16), :
                ]
        out[...] = turned[...].T


def per_device(states, window, potential):
    f32 = jnp.float32
    dma = pltpu.SemaphoreType.DMA
    vmem = pltpu.VMEM
    whole = pl.pallas_call(
        kernel,
        out_shape=jax.ShapeDtypeStruct((16, 16, 128), f32),
        in_specs=[pl.BlockSpec(memory_space=pl.ANY)] * 3,
        out_specs=pl.BlockSpec(memory_space=pltpu.VMEM),
        scratch_shapes=[
            vmem((NZ, SPAN, NY), f32),
            vmem((NZ, SPAN, NY), f32),
            vmem((NZ, SPAN, NY), f32),
            vmem((NZ, 32, NY), f32),
            vmem((2, 128, 4, TILE, NY), f32),
            vmem((CELLS, 256), jnp.bfloat16),
            vmem((CELLS, 256), jnp.bfloat16),
            vmem((16, 2, XN, 2, 4, TILE, NY), f32),
            vmem((128, CELLS), jnp.bfloat16),
            vmem((16, 16, 256), f32),
            vmem((32, 16, 128), f32),
            vmem((16, 16, 128), f32),
            vmem((XN, 2, 16, 128), f32),
            vmem((HN, 16, 128), f32),
            dma((12,)), dma((12,)), dma((12,)), dma((12,)), dma((3,)), dma((3,)),
            dma((5,)), dma, dma,
            dma((2, XN, 2)), dma((2, XN, 2)),
            dma((16, 2, XN)), dma((16, 2, XN)), dma((16, 2, XN)), dma((16, 2, XN)),
            dma((16, 2)), dma((32,)), dma((16,)), dma((16,)),
            dma((XN, 2)), dma((XN, 2)), dma((HN,)), dma((HN,)),
        ],
        compiler_params=pltpu.CompilerParams(
            collective_id=0, has_side_effects=True, vmem_limit_bytes=60 * 1024 * 1024
        ),
    )(states, window, potential)
    return pl.pallas_call(
        finish,
        out_shape=(
            jax.ShapeDtypeStruct((128, 128), f32),
            jax.ShapeDtypeStruct((128, 128), f32),
        ),
        in_specs=[pl.BlockSpec(memory_space=pltpu.VMEM)],
        out_specs=(pl.BlockSpec(memory_space=pltpu.VMEM),) * 2,
        scratch_shapes=[vmem((128, 128), f32)],
    )(whole)


def solution(mesh):
    in_specs = (P("band", None, "dom", None), P("band", None, "dom", None), P(None, "dom", None))
    out_specs = (P("band", None), P("band", None))
    return jax.shard_map(
        per_device, mesh=mesh, in_specs=in_specs, out_specs=out_specs, check_vma=False
    )
```

```python
import jax
import jax.numpy as jnp
from jax import lax
from jax.experimental import pallas as pl
from jax.experimental.pallas import tpu as pltpu
from jax.sharding import PartitionSpec as P

COEFFS = (
    -5369.0 / 1800.0,
    12.0 / 7.0,
    -15.0 / 56.0,
    10.0 / 189.0,
    -1.0 / 112.0,
    2.0 / 1925.0,
    -1.0 / 16632.0,
)
CENTRE = 9.0
HALF_WIDTH = 7.0
MESH = pl.DeviceIdType.MESH
NY = 128
NZ = 8
TILE = 8
XN = 4
HN = 4
YN = 8
SPAN = 96
CELLS = 4096


def apply_h(source, potential, z, low, high):
    value = source[z, low:high, :]
    total = (3.0 * COEFFS[0]) * value
    for k in range(1, 7):
        beside = source[z, low + k : high + k, :] + source[z, low - k : high - k, :]
        beside = beside + pltpu.roll(value, k, 1) + pltpu.roll(value, NY - k, 1)
        if z + k < NZ:
            beside = beside + source[z + k, low:high, :]
        if z - k >= 0:
            beside = beside + source[z - k, low:high, :]
        total = total + COEFFS[k] * beside
    if potential is None:
        return -0.5 * total, value
    return -0.5 * total + potential[z, low:high, :] * value, value


def kernel(
    states, window, potential, out,
    even, odd, pot, image, rows, high, low, gathered, left, partial, parts, whole, near, far,
    send_w, recv_w, send_p, recv_p, send_t, recv_t, local, send_s, recv_s, send_b, recv_b,
    send_up, send_down, send_z, recv_g, send_r, recv_r, send_o, recv_o,
    send_near, recv_near, send_far, recv_far,
):
    b = lax.axis_index("band")
    d = lax.axis_index("dom")
    c = lax.rem(b, 2)
    q = lax.div(b, 2)
    y = lax.rem(q, YN)
    zl = lax.div(q, YN)
    x = lax.rem(d, XN)
    h = lax.div(d, XN)

    def band_of(chip, core):
        return chip * 2 + core

    def chip_at(lo, offset):
        return lo * YN + lax.rem(y + offset + YN, YN)

    up = band_of(chip_at(zl, 1), c)
    down = band_of(chip_at(zl, -1), c)
    across = band_of((1 - zl) * YN + y, c)
    twin = band_of(q, 1 - c)
    columns = [lax.rem(x + k, XN) for k in range(XN)]

    def remote(src, dst, send, recv, band, dom):
        return pltpu.make_async_remote_copy(
            src_ref=src, dst_ref=dst, send_sem=send, recv_sem=recv,
            device_id=(band, dom), device_id_type=MESH,
        )

    wide = []
    for side in (-1, 1, 0):
        row = lax.rem(h + side + HN, HN)
        for k in range(XN):
            if side != 0 or k != 0:
                wide.append((side, row, columns[k]))
    barrier = pltpu.get_barrier_semaphore()

    def greet(band, dom):
        pl.semaphore_signal(barrier, inc=1, device_id=(band, dom), device_id_type=MESH)

    for side, row, column in wide:
        greet(b, row * XN + column)
    for k in range(XN):
        greet(twin, h * XN + columns[k])
    for band in (up, down, across):
        greet(band, d)
    pl.semaphore_wait(barrier, 18)

    started = []

    def begin(copy):
        copy.start()
        started.append(copy)

    def planes(side, slot_x):
        return pl.ds(pl.multiple_of(((1 - side) * XN + slot_x) * TILE, TILE), TILE)

    mine = pl.ds(4 * c, 4)

    def met(side, column):
        if side == 1:
            return column != 0
        return column != XN - 1

    guarded = []
    for n, (side, row, column) in enumerate(wide):
        copy = remote(
            potential.at[mine], pot.at[mine, planes(side, x), :],
            send_p.at[n], recv_p.at[(1 - side) * XN + x], b, row * XN + column,
        )
        if side == 0:
            begin(copy)
        else:
            sent = met(side, x)
            pl.when(sent)(copy.start)
            guarded.append((sent, copy))
    for n, (side, row, column) in enumerate(wide):
        begin(
            remote(
                window.at[column], even.at[:, planes(side, x), :],
                send_w.at[n], recv_w.at[(1 - side) * XN + x], b, row * XN + column,
            )
        )
    own = [
        pltpu.make_async_copy(window.at[x], even.at[:, planes(0, x), :], local.at[1]),
        pltpu.make_async_copy(potential.at[mine], pot.at[mine, planes(0, x), :], local.at[2]),
    ]
    for copy in own:
        copy.start()
    keep = pltpu.make_async_copy(states.at[:, mine], rows.at[c], local.at[0])
    keep.start()
    swap = remote(states.at[:, pl.ds(4 * (1 - c), 4)], rows.at[c], send_s, recv_s, twin, d)
    begin(swap)

    flat_rows = rows.reshape(2 * 128 * 32, NY)

    def split_states(core):
        def body(turn, carry):
            for n in range(4):
                k = 4 * turn + n
                value = flat_rows[pl.ds(core * 4096 + k, 128, stride=32), :].T
                upper = value.astype(jnp.bfloat16)
                cells = pl.ds(pl.multiple_of(k * NY, NY), NY)
                lanes = pl.ds(pl.multiple_of(core * 128, 128), 128)
                high[cells, lanes] = upper
                low[cells, lanes] = (value - upper.astype(jnp.float32)).astype(jnp.bfloat16)
            return carry

        lax.fori_loop(0, 8, body, 0)

    keep.wait()
    split_states(c)
    swap.wait_recv()
    split_states(1 - c)

    own[1].wait()
    for n, side in enumerate((-1, 1, 0)):
        for place, row, column in wide:
            if place != side:
                continue
            copy = remote(
                potential.at[mine], pot.at[mine, planes(side, column), :],
                send_p.at[0], recv_p.at[(1 - side) * XN + column], b, d,
            )
            if side == 0:
                copy.wait_recv()
            else:
                pl.when(met(side, column))(copy.wait_recv)
        low_row, high_row = {1: (8, 32), 0: (32, 64), -1: (64, 88)}[side]
        strip = pot.at[mine, pl.ds(low_row, high_row - low_row), :]
        begin(remote(strip, strip, send_t.at[n], recv_t.at[n], twin, d))

    own[0].wait()
    for side, row, column in wide:
        remote(
            window.at[0], even.at[:, planes(side, column), :],
            send_w.at[0], recv_w.at[(1 - side) * XN + column], b, d,
        ).wait_recv()

    for z in range(NZ):
        product, value = apply_h(even, None, z, 8, 88)
        odd[z, 8:88, :] = (product - CENTRE * value) * (1.0 / HALF_WIDTH)
    for n, side in enumerate((-1, 1, 0)):
        low_row, high_row = {1: (8, 32), 0: (32, 64), -1: (64, 88)}[side]
        strip = pot.at[pl.ds(4 * (1 - c), 4), pl.ds(low_row, high_row - low_row), :]
        remote(strip, strip, send_t.at[n], recv_t.at[n], twin, d).wait_recv()
    for z in range(NZ):
        odd[z, 8:88, :] += pot[z, 8:88, :] * even[z, 8:88, :] * (1.0 / HALF_WIDTH)
    for source, target, first, last in ((odd, even, 8, 88), (even, odd, 16, 80), (odd, even, 24, 72)):
        for z in range(NZ):
            product, value = apply_h(source, pot, z, first, last)
            target[z, first:last, :] = (
                (product - CENTRE * value) * (2.0 / HALF_WIDTH) - target[z, first:last, :]
            )

    own_pieces = []

    def hand_on(kind, source, offset):
        for k in (0, 2, 1, 3):
            for j in range(2):
                core = lax.rem(c + j, 2)
                place = pl.ds(pl.multiple_of(offset + TILE * columns[k], TILE), TILE)
                piece = source.at[pl.ds(4 * core, 4), place, :]
                goal = gathered.at[q, kind, x, c]
                if k == 0 and j == 0:
                    copy = pltpu.make_async_copy(piece, goal, local.at[3 + kind])
                    copy.start()
                    own_pieces.append(copy)
                else:
                    begin(
                        remote(
                            piece, goal, send_b.at[kind, k, j], recv_b.at[kind, x, c],
                            band_of(q, core), h * XN + columns[k],
                        )
                    )

    hand_on(0, even, 32)
    for z in range(NZ):
        product, value = apply_h(even, pot, z, 32, 64)
        image[z] = product
    hand_on(1, image, 0)

    def forward(chip, kind, k, sems, band):
        place = gathered.at[chip, kind, columns[k]]
        begin(
            remote(place, place, sems.at[chip, kind, k], recv_g.at[chip, kind, k], band, d)
        )

    def arrive(chip, kind, k):
        place = gathered.at[chip, kind, columns[k]]
        remote(
            place, place, send_z.at[chip, kind, k], recv_g.at[chip, kind, k], across, d
        ).wait_recv()

    order = ((0, 0), (0, 1), (0, 3), (1, 0), (0, 2), (1, 1), (1, 3), (1, 2))
    for kind, k in order:
        for j in range(2):
            if k == 0 and j == 0:
                own_pieces[kind].wait()
                continue
            core = lax.rem(c + j, 2)
            remote(
                image.at[pl.ds(0, 4), pl.ds(0, TILE), :], gathered.at[q, kind, columns[k], core],
                send_b.at[0, 0, 0], recv_b.at[kind, columns[k], core], b, d,
            ).wait_recv()
        if kind == 0:
            forward(q, 0, k, send_z, across)
        forward(q, kind, k, send_up, up)
        forward(q, kind, k, send_down, down)
        if kind == 1:
            forward(q, 1, k, send_z, across)

    other = chip_at(1 - zl, 0)
    for k in (0, 1, 3, 2):
        arrive(other, 0, k)
        forward(other, 0, k, send_up, up)
        forward(other, 0, k, send_down, down)

    flat_pieces = gathered.reshape(16 * 512, NY)

    def multiply(chips, last=False):
        count = 16 * len(chips)
        for n, chip in enumerate(chips):
            for k in range(32):
                lanes = slice(NY * k, NY * (k + 1))
                value = flat_pieces[pl.ds(chip * 512 + k, 16, stride=32), :]
                upper = value.astype(jnp.bfloat16)
                left[16 * n : 16 * n + 16, lanes] = upper
                left[count + 16 * n : count + 16 * n + 16, lanes] = (
                    value - upper.astype(jnp.float32)
                ).astype(jnp.bfloat16)
        both = jnp.dot(left[0 : 2 * count, :], high[...], preferred_element_type=jnp.float32)
        rest = jnp.dot(left[0:count, :], low[...], preferred_element_type=jnp.float32)
        product = both[0:count] + (both[count:] + rest)
        for n, chip in enumerate(chips):
            partial[chip] = product[16 * n : 16 * n + 16]
            if last:
                continue
            for core in range(2):
                copy = remote(
                    partial.at[chip, :, pl.ds(128 * core, 128)], parts.at[d * 2 + c],
                    send_r.at[chip, core], recv_r.at[d * 2 + c], band_of(q, core), chip,
                )
                away = jnp.logical_or(chip != d, c != core)
                pl.when(away)(copy.start)
                guarded.append((away, copy))

    def reduce_own():
        def take(source, total):
            remote(
                partial.at[0, :, pl.ds(0, 128)], parts.at[source],
                send_r.at[0, 0], recv_r.at[source], b, d,
            ).wait_recv()
            return total + parts[source]

        total = partial[d, :, pl.ds(pl.multiple_of(128 * c, 128), 128)]
        total = lax.fori_loop(
            0, 16, lambda k, t: take(lax.rem(d + k, 16) * 2 + (1 - c), t), total
        )
        total = lax.fori_loop(1, 16, lambda k, t: take(lax.rem(d + k, 16) * 2 + c, t), total)
        whole[d] = total
        for k in range(1, 16):
            remote(
                whole.at[d], whole.at[d], send_o.at[k], recv_o.at[d], b, lax.rem(d + k, 16)
            ).start()

    ahead = lax.rem(lax.rem(d, YN) - y + YN, YN)
    final = chip_at(1 - zl, 4)
    turn = jnp.where(d == final, 5, jnp.maximum(jnp.minimum(ahead, YN - ahead), 1))
    images = ((zl, 1),)
    filtered = ((zl, 0), (1 - zl, 0))

    def ring_step(step, kinds):
        for lo, kind, k in [(lo, kind, k) for lo, kind in kinds for k in (0, 1, 3, 2)]:
            for direction in (1, -1):
                keeps = (k < 2) == (direction == 1)
                if step == 4 and not keeps:
                    continue
                chip = chip_at(lo, -direction * step)
                arrive(chip, kind, k)
                if step < 3 or (step == 3 and keeps):
                    if direction == 1:
                        forward(chip, kind, k, send_up, up)
                    else:
                        forward(chip, kind, k, send_down, down)
                if kind == 1:
                    forward(chip, kind, k, send_z, across)

    def cross(offset):
        for k in (0, 1, 3, 2):
            arrive(chip_at(1 - zl, offset), 1, k)

    for step in range(1, 4):
        ring_step(step, images + filtered)
        if step == 3:
            ring_step(4, images)
        offsets = [step, -step] if step > 1 else [0, step, -step]
        for offset in offsets:
            cross(offset)
        multiply([chip_at(lo, o) for lo in (zl, 1 - zl) for o in offsets])
        if step > 1:
            pl.when(turn == step - 1)(reduce_own)
    ring_step(4, filtered)
    multiply([chip_at(zl, 4)])
    cross(4)
    multiply([final], last=True)
    for k in (2, 1, 3, 0):
        for j in range(2):
            core = lax.rem(c + j, 2)
            part = partial.at[final, :, pl.ds(pl.multiple_of(128 * core, 128), 128)]
            if k == 0 and j == 0:
                near[x, c] = part[...]
            else:
                begin(
                    remote(
                        part, near.at[x, c], send_near.at[k, j], recv_near.at[x, c],
                        band_of(q, core), h * XN + columns[k],
                    )
                )
    for k in range(XN):
        for j in range(2):
            if k != 0 or j != 0:
                core = lax.rem(c + j, 2)
                remote(
                    near.at[x, c], near.at[columns[k], core], send_near.at[0, 1],
                    recv_near.at[columns[k], core], b, d,
                ).wait_recv()
    total = near[0, 0] + near[0, 1]
    for column in range(1, XN):
        total = total + (near[column, 0] + near[column, 1])
    far[h] = total
    for k in (2, 1, 3):
        begin(
            remote(
                far.at[h], far.at[h], send_far.at[k], recv_far.at[h],
                b, lax.rem(h + k, HN) * XN + x,
            )
        )
    pl.when(jnp.logical_or(turn == 3, turn == 4))(reduce_own)
    for k in range(1, 16):
        source = lax.rem(d + k, 16)
        copy = remote(whole.at[source], whole.at[source], send_o.at[k], recv_o.at[source], b, d)
        pl.when(source != final)(copy.wait_recv)
    for k in range(1, HN):
        row = lax.rem(h + k, HN)
        remote(far.at[h], far.at[row], send_far.at[k], recv_far.at[row], b, d).wait_recv()
    whole[final] = (far[0] + far[1]) + (far[2] + far[3])
    out[...] = whole[...]

    for copy in started:
        copy.wait_send()
    for sent, copy in guarded:
        pl.when(sent)(copy.wait_send)
    for k in range(1, 16):
        copy = remote(whole.at[d], whole.at[d], send_o.at[k], recv_o.at[d], b, lax.rem(d + k, 16))
        pl.when(d != final)(copy.wait_send)


def finish(whole, out_f, out_h, turned):
    flat = whole.reshape(256, 128)
    for kind, out in ((0, out_f), (1, out_h)):
        for column in range(XN):
            for core in range(2):
                turned[pl.ds(4 * core + column, 16, stride=8), :] = flat[
                    pl.ds(8 * kind + 2 * column + core, 16, stride=16), :
                ]
        out[...] = turned[...].T


def per_device(states, window, potential):
    f32 = jnp.float32
    dma = pltpu.SemaphoreType.DMA
    vmem = pltpu.VMEM
    whole = pl.pallas_call(
        kernel,
        out_shape=jax.ShapeDtypeStruct((16, 16, 128), f32),
        in_specs=[pl.BlockSpec(memory_space=pl.ANY)] * 3,
        out_specs=pl.BlockSpec(memory_space=pltpu.VMEM),
        scratch_shapes=[
            vmem((NZ, SPAN, NY), f32),
            vmem((NZ, SPAN, NY), f32),
            vmem((NZ, SPAN, NY), f32),
            vmem((NZ, 32, NY), f32),
            vmem((2, 128, 4, TILE, NY), f32),
            vmem((CELLS, 256), jnp.bfloat16),
            vmem((CELLS, 256), jnp.bfloat16),
            vmem((16, 2, XN, 2, 4, TILE, NY), f32),
            vmem((192, CELLS), jnp.bfloat16),
            vmem((16, 16, 256), f32),
            vmem((32, 16, 128), f32),
            vmem((16, 16, 128), f32),
            vmem((XN, 2, 16, 128), f32),
            vmem((HN, 16, 128), f32),
            dma((12,)), dma((12,)), dma((12,)), dma((12,)), dma((3,)), dma((3,)),
            dma((5,)), dma, dma,
            dma((2, XN, 2)), dma((2, XN, 2)),
            dma((16, 2, XN)), dma((16, 2, XN)), dma((16, 2, XN)), dma((16, 2, XN)),
            dma((16, 2)), dma((32,)), dma((16,)), dma((16,)),
            dma((XN, 2)), dma((XN, 2)), dma((HN,)), dma((HN,)),
        ],
        compiler_params=pltpu.CompilerParams(
            collective_id=0, has_side_effects=True, vmem_limit_bytes=60 * 1024 * 1024
        ),
    )(states, window, potential)
    return pl.pallas_call(
        finish,
        out_shape=(
            jax.ShapeDtypeStruct((128, 128), f32),
            jax.ShapeDtypeStruct((128, 128), f32),
        ),
        in_specs=[pl.BlockSpec(memory_space=pltpu.VMEM)],
        out_specs=(pl.BlockSpec(memory_space=pltpu.VMEM),) * 2,
        scratch_shapes=[vmem((128, 128), f32)],
    )(whole)


def solution(mesh):
    in_specs = (P("band", None, "dom", None), P("band", None, "dom", None), P(None, "dom", None))
    out_specs = (P("band", None), P("band", None))
    return jax.shard_map(
        per_device, mesh=mesh, in_specs=in_specs, out_specs=out_specs, check_vma=False
    )
```

```python
import jax
import jax.numpy as jnp
from jax import lax
from jax.experimental import pallas as pl
from jax.experimental.pallas import tpu as pltpu
from jax.sharding import PartitionSpec as P

COEFFS = (
    -5369.0 / 1800.0,
    12.0 / 7.0,
    -15.0 / 56.0,
    10.0 / 189.0,
    -1.0 / 112.0,
    2.0 / 1925.0,
    -1.0 / 16632.0,
)
CENTRE = 9.0
HALF_WIDTH = 7.0
MESH = pl.DeviceIdType.MESH
NY = 128
NZ = 8
TILE = 8
XN = 4
HN = 4
YN = 8
SPAN = 96
CELLS = 4096


def apply_h(source, potential, z, low, high):
    value = source[z, low:high, :]
    total = (3.0 * COEFFS[0]) * value
    for k in range(1, 7):
        beside = source[z, low + k : high + k, :] + source[z, low - k : high - k, :]
        beside = beside + pltpu.roll(value, k, 1) + pltpu.roll(value, NY - k, 1)
        if z + k < NZ:
            beside = beside + source[z + k, low:high, :]
        if z - k >= 0:
            beside = beside + source[z - k, low:high, :]
        total = total + COEFFS[k] * beside
    if potential is None:
        return -0.5 * total, value
    return -0.5 * total + potential[z, low:high, :] * value, value


def kernel(
    states, window, potential, out,
    even, odd, pot, image, rows, high, low, gathered, left, partial, parts, whole, near, far,
    send_w, recv_w, send_p, recv_p, send_t, recv_t, local, send_s, recv_s, send_b, recv_b,
    send_up, send_down, send_z, recv_g, send_r, recv_r, send_o, recv_o,
    send_near, recv_near, send_far, recv_far,
):
    b = lax.axis_index("band")
    d = lax.axis_index("dom")
    c = lax.rem(b, 2)
    q = lax.div(b, 2)
    y = lax.rem(q, YN)
    zl = lax.div(q, YN)
    x = lax.rem(d, XN)
    h = lax.div(d, XN)

    def band_of(chip, core):
        return chip * 2 + core

    def chip_at(lo, offset):
        return lo * YN + lax.rem(y + offset + YN, YN)

    up = band_of(chip_at(zl, 1), c)
    down = band_of(chip_at(zl, -1), c)
    across = band_of((1 - zl) * YN + y, c)
    twin = band_of(q, 1 - c)
    columns = [lax.rem(x + k, XN) for k in range(XN)]

    def remote(src, dst, send, recv, band, dom):
        return pltpu.make_async_remote_copy(
            src_ref=src, dst_ref=dst, send_sem=send, recv_sem=recv,
            device_id=(band, dom), device_id_type=MESH,
        )

    wide = []
    for side in (-1, 1, 0):
        row = lax.rem(h + side + HN, HN)
        for k in range(XN):
            if side != 0 or k != 0:
                wide.append((side, row, columns[k]))
    barrier = pltpu.get_barrier_semaphore()

    def greet(band, dom):
        pl.semaphore_signal(barrier, inc=1, device_id=(band, dom), device_id_type=MESH)

    for side, row, column in wide:
        greet(b, row * XN + column)
    for k in range(XN):
        greet(twin, h * XN + columns[k])
    for band in (up, down, across):
        greet(band, d)
    pl.semaphore_wait(barrier, 18)

    started = []

    def begin(copy):
        copy.start()
        started.append(copy)

    def planes(side, slot_x):
        return pl.ds(pl.multiple_of(((1 - side) * XN + slot_x) * TILE, TILE), TILE)

    mine = pl.ds(4 * c, 4)

    def met(side, column):
        if side == 1:
            return column != 0
        return column != XN - 1

    guarded = []
    for n, (side, row, column) in enumerate(wide):
        copy = remote(
            potential.at[mine], pot.at[mine, planes(side, x), :],
            send_p.at[n], recv_p.at[(1 - side) * XN + x], b, row * XN + column,
        )
        if side == 0:
            begin(copy)
        else:
            sent = met(side, x)
            pl.when(sent)(copy.start)
            guarded.append((sent, copy))
    for n, (side, row, column) in enumerate(wide):
        begin(
            remote(
                window.at[column], even.at[:, planes(side, x), :],
                send_w.at[n], recv_w.at[(1 - side) * XN + x], b, row * XN + column,
            )
        )
    own = [
        pltpu.make_async_copy(window.at[x], even.at[:, planes(0, x), :], local.at[1]),
        pltpu.make_async_copy(potential.at[mine], pot.at[mine, planes(0, x), :], local.at[2]),
    ]
    for copy in own:
        copy.start()
    keep = pltpu.make_async_copy(states.at[:, mine], rows.at[c], local.at[0])
    keep.start()
    swap = remote(states.at[:, pl.ds(4 * (1 - c), 4)], rows.at[c], send_s, recv_s, twin, d)
    begin(swap)

    flat_rows = rows.reshape(2 * 128 * 32, NY)

    def split_states(core):
        def body(turn, carry):
            for n in range(4):
                k = 4 * turn + n
                value = flat_rows[pl.ds(core * 4096 + k, 128, stride=32), :].T
                upper = value.astype(jnp.bfloat16)
                cells = pl.ds(pl.multiple_of(k * NY, NY), NY)
                lanes = pl.ds(pl.multiple_of(core * 128, 128), 128)
                high[cells, lanes] = upper
                low[cells, lanes] = (value - upper.astype(jnp.float32)).astype(jnp.bfloat16)
            return carry

        lax.fori_loop(0, 8, body, 0)

    keep.wait()
    split_states(c)
    swap.wait_recv()
    split_states(1 - c)

    own[1].wait()
    for n, side in enumerate((-1, 1, 0)):
        for place, row, column in wide:
            if place != side:
                continue
            copy = remote(
                potential.at[mine], pot.at[mine, planes(side, column), :],
                send_p.at[0], recv_p.at[(1 - side) * XN + column], b, d,
            )
            if side == 0:
                copy.wait_recv()
            else:
                pl.when(met(side, column))(copy.wait_recv)
        low_row, high_row = {1: (8, 32), 0: (32, 64), -1: (64, 88)}[side]
        strip = pot.at[mine, pl.ds(low_row, high_row - low_row), :]
        begin(remote(strip, strip, send_t.at[n], recv_t.at[n], twin, d))

    own[0].wait()
    for side, row, column in wide:
        remote(
            window.at[0], even.at[:, planes(side, column), :],
            send_w.at[0], recv_w.at[(1 - side) * XN + column], b, d,
        ).wait_recv()

    for z in range(NZ):
        product, value = apply_h(even, None, z, 8, 88)
        odd[z, 8:88, :] = (product - CENTRE * value) * (1.0 / HALF_WIDTH)
    for n, side in enumerate((-1, 1, 0)):
        low_row, high_row = {1: (8, 32), 0: (32, 64), -1: (64, 88)}[side]
        strip = pot.at[pl.ds(4 * (1 - c), 4), pl.ds(low_row, high_row - low_row), :]
        remote(strip, strip, send_t.at[n], recv_t.at[n], twin, d).wait_recv()
    for z in range(NZ):
        odd[z, 8:88, :] += pot[z, 8:88, :] * even[z, 8:88, :] * (1.0 / HALF_WIDTH)
    for source, target, first, last in ((odd, even, 8, 88), (even, odd, 16, 80), (odd, even, 24, 72)):
        for z in range(NZ):
            product, value = apply_h(source, pot, z, first, last)
            target[z, first:last, :] = (
                (product - CENTRE * value) * (2.0 / HALF_WIDTH) - target[z, first:last, :]
            )

    own_pieces = []

    def hand_on(kind, source, offset):
        for k in (0, 2, 1, 3):
            for j in range(2):
                core = lax.rem(c + j, 2)
                place = pl.ds(pl.multiple_of(offset + TILE * columns[k], TILE), TILE)
                piece = source.at[pl.ds(4 * core, 4), place, :]
                goal = gathered.at[q, kind, x, c]
                if k == 0 and j == 0:
                    copy = pltpu.make_async_copy(piece, goal, local.at[3 + kind])
                    copy.start()
                    own_pieces.append(copy)
                else:
                    begin(
                        remote(
                            piece, goal, send_b.at[kind, k, j], recv_b.at[kind, x, c],
                            band_of(q, core), h * XN + columns[k],
                        )
                    )

    hand_on(0, even, 32)
    for z in range(NZ):
        product, value = apply_h(even, pot, z, 32, 64)
        image[z] = product
    hand_on(1, image, 0)

    def forward(chip, kind, k, sems, band):
        place = gathered.at[chip, kind, columns[k]]
        begin(
            remote(place, place, sems.at[chip, kind, k], recv_g.at[chip, kind, k], band, d)
        )

    def arrive(chip, kind, k):
        place = gathered.at[chip, kind, columns[k]]
        remote(
            place, place, send_z.at[chip, kind, k], recv_g.at[chip, kind, k], across, d
        ).wait_recv()

    order = ((0, 0), (0, 1), (0, 3), (1, 0), (0, 2), (1, 1), (1, 3), (1, 2))
    for kind, k in order:
        for j in range(2):
            if k == 0 and j == 0:
                own_pieces[kind].wait()
                continue
            core = lax.rem(c + j, 2)
            remote(
                image.at[pl.ds(0, 4), pl.ds(0, TILE), :], gathered.at[q, kind, columns[k], core],
                send_b.at[0, 0, 0], recv_b.at[kind, columns[k], core], b, d,
            ).wait_recv()
        if kind == 0:
            forward(q, 0, k, send_z, across)
        forward(q, kind, k, send_up, up)
        forward(q, kind, k, send_down, down)
        if kind == 1:
            forward(q, 1, k, send_z, across)

    other = chip_at(1 - zl, 0)
    for k in (0, 1, 3, 2):
        arrive(other, 0, k)
        forward(other, 0, k, send_up, up)
        forward(other, 0, k, send_down, down)

    flat_pieces = gathered.reshape(16 * 512, NY)

    def multiply(chips, last=False):
        count = 16 * len(chips)
        for n, chip in enumerate(chips):
            for k in range(32):
                lanes = slice(NY * k, NY * (k + 1))
                value = flat_pieces[pl.ds(chip * 512 + k, 16, stride=32), :]
                upper = value.astype(jnp.bfloat16)
                left[16 * n : 16 * n + 16, lanes] = upper
                left[count + 16 * n : count + 16 * n + 16, lanes] = (
                    value - upper.astype(jnp.float32)
                ).astype(jnp.bfloat16)
        both = jnp.dot(left[0 : 2 * count, :], high[...], preferred_element_type=jnp.float32)
        rest = jnp.dot(left[0:count, :], low[...], preferred_element_type=jnp.float32)
        product = both[0:count] + (both[count:] + rest)
        for n, chip in enumerate(chips):
            partial[chip] = product[16 * n : 16 * n + 16]
            if last:
                continue
            for core in range(2):
                copy = remote(
                    partial.at[chip, :, pl.ds(128 * core, 128)], parts.at[d * 2 + c],
                    send_r.at[chip, core], recv_r.at[d * 2 + c], band_of(q, core), chip,
                )
                away = jnp.logical_or(chip != d, c != core)
                pl.when(away)(copy.start)
                guarded.append((away, copy))

    def reduce_own():
        def take(source, total):
            remote(
                partial.at[0, :, pl.ds(0, 128)], parts.at[source],
                send_r.at[0, 0], recv_r.at[source], b, d,
            ).wait_recv()
            return total + parts[source]

        total = partial[d, :, pl.ds(pl.multiple_of(128 * c, 128), 128)]
        total = lax.fori_loop(
            0, 16, lambda k, t: take(lax.rem(d + k, 16) * 2 + (1 - c), t), total
        )
        total = lax.fori_loop(1, 16, lambda k, t: take(lax.rem(d + k, 16) * 2 + c, t), total)
        whole[d] = total
        for k in range(1, 16):
            remote(
                whole.at[d], whole.at[d], send_o.at[k], recv_o.at[d], b, lax.rem(d + k, 16)
            ).start()

    ahead = lax.rem(lax.rem(d, YN) - y + YN, YN)
    final = chip_at(1 - zl, 4)
    facing = chip_at(zl, 4)
    apart = jnp.minimum(ahead, YN - ahead)
    turn = jnp.where(lax.div(d, YN) == zl, jnp.maximum(apart, 1), jnp.minimum(apart + 1, 3))
    turn = jnp.where(apart == 4, 5, turn)
    images = ((zl, 1),)
    filtered = ((zl, 0), (1 - zl, 0))

    def ring_step(step, kinds):
        for lo, kind, k in [(lo, kind, k) for lo, kind in kinds for k in (0, 1, 3, 2)]:
            for direction in (1, -1):
                keeps = (k < 2) == (direction == 1)
                if step == 4 and not keeps:
                    continue
                chip = chip_at(lo, -direction * step)
                arrive(chip, kind, k)
                if step < 3 or (step == 3 and keeps):
                    if direction == 1:
                        forward(chip, kind, k, send_up, up)
                    else:
                        forward(chip, kind, k, send_down, down)
                if kind == 1:
                    forward(chip, kind, k, send_z, across)

    def cross(offset):
        for k in (0, 1, 3, 2):
            arrive(chip_at(1 - zl, offset), 1, k)

    for step in range(1, 4):
        ring_step(step, images + filtered)
        if step == 3:
            ring_step(4, images)
        level = [0, 1, -1] if step == 1 else [step, -step]
        behind = {1: [0], 2: [1, -1], 3: [2, -2, 3, -3]}[step]
        for offset in behind:
            cross(offset)
        multiply([chip_at(zl, o) for o in level] + [chip_at(1 - zl, o) for o in behind])
        if step > 1:
            pl.when(turn == step - 1)(reduce_own)

    def near_start(n, chip):
        for k in (2, 1, 3, 0):
            for j in range(2):
                core = lax.rem(c + j, 2)
                part = partial.at[chip, :, pl.ds(pl.multiple_of(128 * core, 128), 128)]
                if k == 0 and j == 0:
                    near[n, x, c] = part[...]
                else:
                    begin(
                        remote(
                            part, near.at[n, x, c], send_near.at[n, k, j], recv_near.at[n, x, c],
                            band_of(q, core), h * XN + columns[k],
                        )
                    )

    def near_finish(n):
        for k in range(XN):
            for j in range(2):
                if k != 0 or j != 0:
                    core = lax.rem(c + j, 2)
                    remote(
                        near.at[n, x, c], near.at[n, columns[k], core], send_near.at[n, 0, 1],
                        recv_near.at[n, columns[k], core], b, d,
                    ).wait_recv()
        total = near[n, 0, 0] + near[n, 0, 1]
        for column in range(1, XN):
            total = total + (near[n, column, 0] + near[n, column, 1])
        far[n, h] = total
        for k in (2, 1, 3):
            begin(
                remote(
                    far.at[n, h], far.at[n, h], send_far.at[n, k], recv_far.at[n, h],
                    b, lax.rem(h + k, HN) * XN + x,
                )
            )

    ring_step(4, filtered)
    multiply([facing], last=True)
    near_start(0, facing)
    cross(4)
    multiply([final], last=True)
    near_start(1, final)
    near_finish(0)
    pl.when(turn == 3)(reduce_own)
    near_finish(1)
    for k in range(1, 16):
        source = lax.rem(d + k, 16)
        copy = remote(whole.at[source], whole.at[source], send_o.at[k], recv_o.at[source], b, d)
        pl.when(jnp.logical_and(source != final, source != facing))(copy.wait_recv)
    for n, chip in ((0, facing), (1, final)):
        for k in range(1, HN):
            row = lax.rem(h + k, HN)
            remote(
                far.at[n, h], far.at[n, row], send_far.at[n, k], recv_far.at[n, row], b, d
            ).wait_recv()
        whole[chip] = (far[n, 0] + far[n, 1]) + (far[n, 2] + far[n, 3])
    out[...] = whole[...]

    for copy in started:
        copy.wait_send()
    for sent, copy in guarded:
        pl.when(sent)(copy.wait_send)
    for k in range(1, 16):
        copy = remote(whole.at[d], whole.at[d], send_o.at[k], recv_o.at[d], b, lax.rem(d + k, 16))
        pl.when(turn < 5)(copy.wait_send)


def finish(whole, out_f, out_h, turned):
    flat = whole.reshape(256, 128)
    for kind, out in ((0, out_f), (1, out_h)):
        for column in range(XN):
            for core in range(2):
                turned[pl.ds(4 * core + column, 16, stride=8), :] = flat[
                    pl.ds(8 * kind + 2 * column + core, 16, stride=16), :
                ]
        out[...] = turned[...].T


def per_device(states, window, potential):
    f32 = jnp.float32
    dma = pltpu.SemaphoreType.DMA
    vmem = pltpu.VMEM
    whole = pl.pallas_call(
        kernel,
        out_shape=jax.ShapeDtypeStruct((16, 16, 128), f32),
        in_specs=[pl.BlockSpec(memory_space=pl.ANY)] * 3,
        out_specs=pl.BlockSpec(memory_space=pltpu.VMEM),
        scratch_shapes=[
            vmem((NZ, SPAN, NY), f32),
            vmem((NZ, SPAN, NY), f32),
            vmem((NZ, SPAN, NY), f32),
            vmem((NZ, 32, NY), f32),
            vmem((2, 128, 4, TILE, NY), f32),
            vmem((CELLS, 256), jnp.bfloat16),
            vmem((CELLS, 256), jnp.bfloat16),
            vmem((16, 2, XN, 2, 4, TILE, NY), f32),
            vmem((192, CELLS), jnp.bfloat16),
            vmem((16, 16, 256), f32),
            vmem((32, 16, 128), f32),
            vmem((16, 16, 128), f32),
            vmem((2, XN, 2, 16, 128), f32),
            vmem((2, HN, 16, 128), f32),
            dma((12,)), dma((12,)), dma((12,)), dma((12,)), dma((3,)), dma((3,)),
            dma((5,)), dma, dma,
            dma((2, XN, 2)), dma((2, XN, 2)),
            dma((16, 2, XN)), dma((16, 2, XN)), dma((16, 2, XN)), dma((16, 2, XN)),
            dma((16, 2)), dma((32,)), dma((16,)), dma((16,)),
            dma((2, XN, 2)), dma((2, XN, 2)), dma((2, HN)), dma((2, HN)),
        ],
        compiler_params=pltpu.CompilerParams(
            collective_id=0, has_side_effects=True, vmem_limit_bytes=60 * 1024 * 1024
        ),
    )(states, window, potential)
    return pl.pallas_call(
        finish,
        out_shape=(
            jax.ShapeDtypeStruct((128, 128), f32),
            jax.ShapeDtypeStruct((128, 128), f32),
        ),
        in_specs=[pl.BlockSpec(memory_space=pltpu.VMEM)],
        out_specs=(pl.BlockSpec(memory_space=pltpu.VMEM),) * 2,
        scratch_shapes=[vmem((128, 128), f32)],
    )(whole)


def solution(mesh):
    in_specs = (P("band", None, "dom", None), P("band", None, "dom", None), P(None, "dom", None))
    out_specs = (P("band", None), P("band", None))
    return jax.shard_map(
        per_device, mesh=mesh, in_specs=in_specs, out_specs=out_specs, check_vma=False
    )
```

```python
import jax
import jax.numpy as jnp
from jax import lax
from jax.experimental import pallas as pl
from jax.experimental.pallas import tpu as pltpu
from jax.sharding import PartitionSpec as P

COEFFS = (
    -5369.0 / 1800.0,
    12.0 / 7.0,
    -15.0 / 56.0,
    10.0 / 189.0,
    -1.0 / 112.0,
    2.0 / 1925.0,
    -1.0 / 16632.0,
)
CENTRE = 9.0
HALF_WIDTH = 7.0
MESH = pl.DeviceIdType.MESH
NY = 128
NZ = 8
TILE = 8
XN = 4
HN = 4
YN = 8
SPAN = 96
CELLS = 4096


def apply_h(source, potential, z, low, high):
    value = source[z, low:high, :]
    total = (3.0 * COEFFS[0]) * value
    for k in range(1, 7):
        beside = source[z, low + k : high + k, :] + source[z, low - k : high - k, :]
        beside = beside + pltpu.roll(value, k, 1) + pltpu.roll(value, NY - k, 1)
        if z + k < NZ:
            beside = beside + source[z + k, low:high, :]
        if z - k >= 0:
            beside = beside + source[z - k, low:high, :]
        total = total + COEFFS[k] * beside
    if potential is None:
        return -0.5 * total, value
    return -0.5 * total + potential[z, low:high, :] * value, value


def kernel(
    states, window, potential, out,
    even, odd, pot, image, rows, high, low, gathered, left, partial, parts, whole, near, far,
    send_w, recv_w, send_p, recv_p, send_t, recv_t, local, send_s, recv_s, send_b, recv_b,
    send_up, send_down, send_z, recv_g, send_r, recv_r, send_o, recv_o,
    send_near, recv_near, send_far, recv_far,
):
    b = lax.axis_index("band")
    d = lax.axis_index("dom")
    c = lax.rem(b, 2)
    q = lax.div(b, 2)
    y = lax.rem(q, YN)
    zl = lax.div(q, YN)
    x = lax.rem(d, XN)
    h = lax.div(d, XN)

    def band_of(chip, core):
        return chip * 2 + core

    def chip_at(lo, offset):
        return lo * YN + lax.rem(y + offset + YN, YN)

    up = band_of(chip_at(zl, 1), c)
    down = band_of(chip_at(zl, -1), c)
    across = band_of((1 - zl) * YN + y, c)
    twin = band_of(q, 1 - c)
    columns = [lax.rem(x + k, XN) for k in range(XN)]

    def remote(src, dst, send, recv, band, dom):
        return pltpu.make_async_remote_copy(
            src_ref=src, dst_ref=dst, send_sem=send, recv_sem=recv,
            device_id=(band, dom), device_id_type=MESH,
        )

    wide = []
    for side in (-1, 1, 0):
        row = lax.rem(h + side + HN, HN)
        for k in range(XN):
            if side != 0 or k != 0:
                wide.append((side, row, columns[k]))
    barrier = pltpu.get_barrier_semaphore()

    def greet(band, dom):
        pl.semaphore_signal(barrier, inc=1, device_id=(band, dom), device_id_type=MESH)

    for side, row, column in wide:
        greet(b, row * XN + column)
    for k in range(XN):
        greet(twin, h * XN + columns[k])
    for band in (up, down, across):
        greet(band, d)
    pl.semaphore_wait(barrier, 18)

    started = []

    def begin(copy):
        copy.start()
        started.append(copy)

    def planes(side, slot_x):
        return pl.ds(pl.multiple_of(((1 - side) * XN + slot_x) * TILE, TILE), TILE)

    mine = pl.ds(4 * c, 4)

    def met(side, column):
        if side == 1:
            return column != 0
        return column != XN - 1

    guarded = []
    for n, (side, row, column) in enumerate(wide):
        copy = remote(
            potential.at[mine], pot.at[mine, planes(side, x), :],
            send_p.at[n], recv_p.at[(1 - side) * XN + x], b, row * XN + column,
        )
        if side == 0:
            begin(copy)
        else:
            sent = met(side, x)
            pl.when(sent)(copy.start)
            guarded.append((sent, copy))
    for n, (side, row, column) in enumerate(wide):
        if side == 0 or n % XN != 2:
            begin(
                remote(
                    window.at[column], even.at[:, planes(side, x), :],
                    send_w.at[n], recv_w.at[(1 - side) * XN + x], b, row * XN + column,
                )
            )
    own = [
        pltpu.make_async_copy(window.at[x], even.at[:, planes(0, x), :], local.at[1]),
        pltpu.make_async_copy(potential.at[mine], pot.at[mine, planes(0, x), :], local.at[2]),
    ]
    for copy in own:
        copy.start()
    keep = pltpu.make_async_copy(states.at[:, mine], rows.at[c], local.at[0])
    keep.start()
    swap = remote(states.at[:, pl.ds(4 * (1 - c), 4)], rows.at[c], send_s, recv_s, twin, d)
    begin(swap)

    flat_rows = rows.reshape(2 * 128 * 32, NY)

    def split_states(core):
        def body(turn, carry):
            for n in range(4):
                k = 4 * turn + n
                value = flat_rows[pl.ds(core * 4096 + k, 128, stride=32), :].T
                upper = value.astype(jnp.bfloat16)
                cells = pl.ds(pl.multiple_of(k * NY, NY), NY)
                lanes = pl.ds(pl.multiple_of(core * 128, 128), 128)
                high[cells, lanes] = upper
                low[cells, lanes] = (value - upper.astype(jnp.float32)).astype(jnp.bfloat16)
            return carry

        lax.fori_loop(0, 8, body, 0)

    keep.wait()
    split_states(c)
    distant = columns[2]
    tile = even.at[:, planes(0, distant), :]
    remote(window.at[0], tile, send_w.at[0], recv_w.at[XN + distant], b, d).wait_recv()
    passed = []
    for n, side in ((2, -1), (6, 1)):
        copy = remote(
            tile, even.at[:, planes(side, distant), :],
            send_w.at[n], recv_w.at[(1 - side) * XN + distant],
            b, lax.rem(h + side + HN, HN) * XN + x,
        )
        copy.start()
        passed.append(copy)
    swap.wait_recv()
    split_states(1 - c)

    own[1].wait()
    for n, side in enumerate((-1, 1, 0)):
        for place, row, column in wide:
            if place != side:
                continue
            copy = remote(
                potential.at[mine], pot.at[mine, planes(side, column), :],
                send_p.at[0], recv_p.at[(1 - side) * XN + column], b, d,
            )
            if side == 0:
                copy.wait_recv()
            else:
                pl.when(met(side, column))(copy.wait_recv)
        low_row, high_row = {1: (8, 32), 0: (32, 64), -1: (64, 88)}[side]
        strip = pot.at[mine, pl.ds(low_row, high_row - low_row), :]
        begin(remote(strip, strip, send_t.at[n], recv_t.at[n], twin, d))

    own[0].wait()
    for n, (side, row, column) in enumerate(wide):
        if side == 0 and n == 9:
            continue
        remote(
            window.at[0], even.at[:, planes(side, column), :],
            send_w.at[0], recv_w.at[(1 - side) * XN + column], b, d,
        ).wait_recv()

    for z in range(NZ):
        product, value = apply_h(even, None, z, 8, 88)
        odd[z, 8:88, :] = (product - CENTRE * value) * (1.0 / HALF_WIDTH)
    for n, side in enumerate((-1, 1, 0)):
        low_row, high_row = {1: (8, 32), 0: (32, 64), -1: (64, 88)}[side]
        strip = pot.at[pl.ds(4 * (1 - c), 4), pl.ds(low_row, high_row - low_row), :]
        remote(strip, strip, send_t.at[n], recv_t.at[n], twin, d).wait_recv()
    for z in range(NZ):
        odd[z, 8:88, :] += pot[z, 8:88, :] * even[z, 8:88, :] * (1.0 / HALF_WIDTH)
    for copy in passed:
        copy.wait_send()
    for source, target, first, last in ((odd, even, 8, 88), (even, odd, 16, 80), (odd, even, 24, 72)):
        for z in range(NZ):
            product, value = apply_h(source, pot, z, first, last)
            target[z, first:last, :] = (
                (product - CENTRE * value) * (2.0 / HALF_WIDTH) - target[z, first:last, :]
            )

    own_pieces = []

    def hand_on(kind, source, offset):
        for k in (0, 2, 1, 3):
            for j in range(2):
                core = lax.rem(c + j, 2)
                place = pl.ds(pl.multiple_of(offset + TILE * columns[k], TILE), TILE)
                piece = source.at[pl.ds(4 * core, 4), place, :]
                goal = gathered.at[q, kind, x, c]
                if k == 0 and j == 0:
                    copy = pltpu.make_async_copy(piece, goal, local.at[3 + kind])
                    copy.start()
                    own_pieces.append(copy)
                else:
                    begin(
                        remote(
                            piece, goal, send_b.at[kind, k, j], recv_b.at[kind, x, c],
                            band_of(q, core), h * XN + columns[k],
                        )
                    )

    hand_on(0, even, 32)
    for z in range(NZ):
        product, value = apply_h(even, pot, z, 32, 64)
        image[z] = product
    hand_on(1, image, 0)

    def forward(chip, kind, k, sems, band):
        place = gathered.at[chip, kind, columns[k]]
        begin(
            remote(place, place, sems.at[chip, kind, k], recv_g.at[chip, kind, k], band, d)
        )

    def arrive(chip, kind, k):
        place = gathered.at[chip, kind, columns[k]]
        remote(
            place, place, send_z.at[chip, kind, k], recv_g.at[chip, kind, k], across, d
        ).wait_recv()

    order = ((0, 0), (0, 1), (0, 3), (1, 0), (0, 2), (1, 1), (1, 3), (1, 2))
    for kind, k in order:
        for j in range(2):
            if k == 0 and j == 0:
                own_pieces[kind].wait()
                continue
            core = lax.rem(c + j, 2)
            remote(
                image.at[pl.ds(0, 4), pl.ds(0, TILE), :], gathered.at[q, kind, columns[k], core],
                send_b.at[0, 0, 0], recv_b.at[kind, columns[k], core], b, d,
            ).wait_recv()
        if kind == 0:
            forward(q, 0, k, send_z, across)
        forward(q, kind, k, send_up, up)
        forward(q, kind, k, send_down, down)
        if kind == 1:
            forward(q, 1, k, send_z, across)

    other = chip_at(1 - zl, 0)
    for k in (0, 1, 3, 2):
        arrive(other, 0, k)
        forward(other, 0, k, send_up, up)
        forward(other, 0, k, send_down, down)

    flat_pieces = gathered.reshape(16 * 512, NY)

    def multiply(chips, last=False):
        count = 16 * len(chips)
        for n, chip in enumerate(chips):
            for k in range(32):
                lanes = slice(NY * k, NY * (k + 1))
                value = flat_pieces[pl.ds(chip * 512 + k, 16, stride=32), :]
                upper = value.astype(jnp.bfloat16)
                left[16 * n : 16 * n + 16, lanes] = upper
                left[count + 16 * n : count + 16 * n + 16, lanes] = (
                    value - upper.astype(jnp.float32)
                ).astype(jnp.bfloat16)
        both = jnp.dot(left[0 : 2 * count, :], high[...], preferred_element_type=jnp.float32)
        rest = jnp.dot(left[0:count, :], low[...], preferred_element_type=jnp.float32)
        product = both[0:count] + (both[count:] + rest)
        for n, chip in enumerate(chips):
            partial[chip] = product[16 * n : 16 * n + 16]
            if last:
                continue
            for core in range(2):
                copy = remote(
                    partial.at[chip, :, pl.ds(128 * core, 128)], parts.at[d * 2 + c],
                    send_r.at[chip, core], recv_r.at[d * 2 + c], band_of(q, core), chip,
                )
                away = jnp.logical_or(chip != d, c != core)
                pl.when(away)(copy.start)
                guarded.append((away, copy))

    def reduce_own():
        def take(source, total):
            remote(
                partial.at[0, :, pl.ds(0, 128)], parts.at[source],
                send_r.at[0, 0], recv_r.at[source], b, d,
            ).wait_recv()
            return total + parts[source]

        total = partial[d, :, pl.ds(pl.multiple_of(128 * c, 128), 128)]
        total = lax.fori_loop(
            0, 16, lambda k, t: take(lax.rem(d + k, 16) * 2 + (1 - c), t), total
        )
        total = lax.fori_loop(1, 16, lambda k, t: take(lax.rem(d + k, 16) * 2 + c, t), total)
        whole[d] = total
        for k in range(1, 16):
            remote(
                whole.at[d], whole.at[d], send_o.at[k], recv_o.at[d], b, lax.rem(d + k, 16)
            ).start()

    ahead = lax.rem(lax.rem(d, YN) - y + YN, YN)
    final = chip_at(1 - zl, 4)
    facing = chip_at(zl, 4)
    apart = jnp.minimum(ahead, YN - ahead)
    turn = jnp.where(lax.div(d, YN) == zl, jnp.maximum(apart, 1), jnp.minimum(apart + 1, 2))
    turn = jnp.where(apart == 3, 3, jnp.where(apart == 4, 5, turn))
    images = ((zl, 1),)
    filtered = ((zl, 0), (1 - zl, 0))

    def ring_step(step, kinds):
        for lo, kind, k in [(lo, kind, k) for lo, kind in kinds for k in (0, 1, 3, 2)]:
            for direction in (1, -1):
                keeps = (k < 2) == (direction == 1)
                if step == 4 and not keeps:
                    continue
                chip = chip_at(lo, -direction * step)
                arrive(chip, kind, k)
                if step < 3 or (step == 3 and keeps):
                    if direction == 1:
                        forward(chip, kind, k, send_up, up)
                    else:
                        forward(chip, kind, k, send_down, down)
                if kind == 1:
                    forward(chip, kind, k, send_z, across)

    def cross(offset):
        for k in (0, 1, 3, 2):
            arrive(chip_at(1 - zl, offset), 1, k)

    def pair(lo, offset):
        return [chip_at(lo, offset), chip_at(lo, -offset)]

    for step in range(1, 4):
        ring_step(step, images)
        if step > 1:
            cross(step - 1)
            cross(1 - step)
            multiply(pair(1 - zl, step - 1))
        ring_step(step, filtered)
        if step == 1:
            cross(0)
            multiply([q, other] + pair(zl, 1))
            continue
        if step == 3:
            ring_step(4, images)
        multiply(pair(zl, step))
        pl.when(turn == step - 1)(reduce_own)

    def near_start(n, chip):
        for k in (2, 1, 3, 0):
            for j in range(2):
                core = lax.rem(c + j, 2)
                part = partial.at[chip, :, pl.ds(pl.multiple_of(128 * core, 128), 128)]
                if k == 0 and j == 0:
                    near[n, x, c] = part[...]
                else:
                    begin(
                        remote(
                            part, near.at[n, x, c], send_near.at[n, k, j], recv_near.at[n, x, c],
                            band_of(q, core), h * XN + columns[k],
                        )
                    )

    def near_finish(n):
        for k in range(XN):
            for j in range(2):
                if k != 0 or j != 0:
                    core = lax.rem(c + j, 2)
                    remote(
                        near.at[n, x, c], near.at[n, columns[k], core], send_near.at[n, 0, 1],
                        recv_near.at[n, columns[k], core], b, d,
                    ).wait_recv()
        total = near[n, 0, 0] + near[n, 0, 1]
        for column in range(1, XN):
            total = total + (near[n, column, 0] + near[n, column, 1])
        far[n, h] = total
        for k in (2, 1, 3):
            begin(
                remote(
                    far.at[n, h], far.at[n, h], send_far.at[n, k], recv_far.at[n, h],
                    b, lax.rem(h + k, HN) * XN + x,
                )
            )

    cross(3)
    cross(-3)
    multiply(pair(1 - zl, 3))
    ring_step(4, filtered)
    cross(4)
    multiply([facing, final], last=True)
    near_start(0, facing)
    near_start(1, final)
    pl.when(turn == 3)(reduce_own)
    near_finish(0)
    near_finish(1)
    for k in range(1, 16):
        source = lax.rem(d + k, 16)
        copy = remote(whole.at[source], whole.at[source], send_o.at[k], recv_o.at[source], b, d)
        pl.when(jnp.logical_and(source != final, source != facing))(copy.wait_recv)
    for n, chip in ((0, facing), (1, final)):
        for k in range(1, HN):
            row = lax.rem(h + k, HN)
            remote(
                far.at[n, h], far.at[n, row], send_far.at[n, k], recv_far.at[n, row], b, d
            ).wait_recv()
        whole[chip] = (far[n, 0] + far[n, 1]) + (far[n, 2] + far[n, 3])
    out[...] = whole[...]

    for copy in started:
        copy.wait_send()
    for sent, copy in guarded:
        pl.when(sent)(copy.wait_send)
    for k in range(1, 16):
        copy = remote(whole.at[d], whole.at[d], send_o.at[k], recv_o.at[d], b, lax.rem(d + k, 16))
        pl.when(turn < 5)(copy.wait_send)


def finish(whole, out_f, out_h, turned):
    flat = whole.reshape(256, 128)
    for kind, out in ((0, out_f), (1, out_h)):
        for column in range(XN):
            for core in range(2):
                turned[pl.ds(4 * core + column, 16, stride=8), :] = flat[
                    pl.ds(8 * kind + 2 * column + core, 16, stride=16), :
                ]
        out[...] = turned[...].T


def per_device(states, window, potential):
    f32 = jnp.float32
    dma = pltpu.SemaphoreType.DMA
    vmem = pltpu.VMEM
    whole = pl.pallas_call(
        kernel,
        out_shape=jax.ShapeDtypeStruct((16, 16, 128), f32),
        in_specs=[pl.BlockSpec(memory_space=pl.ANY)] * 3,
        out_specs=pl.BlockSpec(memory_space=pltpu.VMEM),
        scratch_shapes=[
            vmem((NZ, SPAN, NY), f32),
            vmem((NZ, SPAN, NY), f32),
            vmem((NZ, SPAN, NY), f32),
            vmem((NZ, 32, NY), f32),
            vmem((2, 128, 4, TILE, NY), f32),
            vmem((CELLS, 256), jnp.bfloat16),
            vmem((CELLS, 256), jnp.bfloat16),
            vmem((16, 2, XN, 2, 4, TILE, NY), f32),
            vmem((192, CELLS), jnp.bfloat16),
            vmem((16, 16, 256), f32),
            vmem((32, 16, 128), f32),
            vmem((16, 16, 128), f32),
            vmem((2, XN, 2, 16, 128), f32),
            vmem((2, HN, 16, 128), f32),
            dma((12,)), dma((12,)), dma((12,)), dma((12,)), dma((3,)), dma((3,)),
            dma((5,)), dma, dma,
            dma((2, XN, 2)), dma((2, XN, 2)),
            dma((16, 2, XN)), dma((16, 2, XN)), dma((16, 2, XN)), dma((16, 2, XN)),
            dma((16, 2)), dma((32,)), dma((16,)), dma((16,)),
            dma((2, XN, 2)), dma((2, XN, 2)), dma((2, HN)), dma((2, HN)),
        ],
        compiler_params=pltpu.CompilerParams(
            collective_id=0, has_side_effects=True, vmem_limit_bytes=60 * 1024 * 1024
        ),
    )(states, window, potential)
    return pl.pallas_call(
        finish,
        out_shape=(
            jax.ShapeDtypeStruct((128, 128), f32),
            jax.ShapeDtypeStruct((128, 128), f32),
        ),
        in_specs=[pl.BlockSpec(memory_space=pltpu.VMEM)],
        out_specs=(pl.BlockSpec(memory_space=pltpu.VMEM),) * 2,
        scratch_shapes=[vmem((128, 128), f32)],
    )(whole)


def solution(mesh):
    in_specs = (P("band", None, "dom", None), P("band", None, "dom", None), P(None, "dom", None))
    out_specs = (P("band", None), P("band", None))
    return jax.shard_map(
        per_device, mesh=mesh, in_specs=in_specs, out_specs=out_specs, check_vma=False
    )
```

```python
import jax
import jax.numpy as jnp
from jax import lax
from jax.experimental import pallas as pl
from jax.experimental.pallas import tpu as pltpu
from jax.sharding import PartitionSpec as P

COEFFS = (
    -5369.0 / 1800.0,
    12.0 / 7.0,
    -15.0 / 56.0,
    10.0 / 189.0,
    -1.0 / 112.0,
    2.0 / 1925.0,
    -1.0 / 16632.0,
)
CENTRE = 9.0
HALF_WIDTH = 7.0
MESH = pl.DeviceIdType.MESH
NY = 128
NZ = 8
TILE = 8
XN = 4
HN = 4
YN = 8
SPAN = 96
CELLS = 4096


def apply_h(source, potential, z, low, high):
    value = source[z, low:high, :]
    total = (3.0 * COEFFS[0]) * value
    for k in range(1, 7):
        beside = source[z, low + k : high + k, :] + source[z, low - k : high - k, :]
        beside = beside + pltpu.roll(value, k, 1) + pltpu.roll(value, NY - k, 1)
        if z + k < NZ:
            beside = beside + source[z + k, low:high, :]
        if z - k >= 0:
            beside = beside + source[z - k, low:high, :]
        total = total + COEFFS[k] * beside
    if potential is None:
        return -0.5 * total, value
    return -0.5 * total + potential[z, low:high, :] * value, value


def kernel(
    states, window, potential, out,
    even, odd, pot, image, rows, high, low, gathered, left, partial, parts, whole, near, far,
    send_w, recv_w, send_p, recv_p, send_t, recv_t, local, send_s, recv_s, send_b, recv_b,
    send_up, send_down, send_z, recv_g, send_r, recv_r, send_o, recv_o,
    send_near, recv_near, send_far, recv_far,
):
    b = lax.axis_index("band")
    d = lax.axis_index("dom")
    c = lax.rem(b, 2)
    q = lax.div(b, 2)
    y = lax.rem(q, YN)
    zl = lax.div(q, YN)
    x = lax.rem(d, XN)
    h = lax.div(d, XN)

    def band_of(chip, core):
        return chip * 2 + core

    def chip_at(lo, offset):
        return lo * YN + lax.rem(y + offset + YN, YN)

    up = band_of(chip_at(zl, 1), c)
    down = band_of(chip_at(zl, -1), c)
    across = band_of((1 - zl) * YN + y, c)
    twin = band_of(q, 1 - c)
    columns = [lax.rem(x + k, XN) for k in range(XN)]

    def remote(src, dst, send, recv, band, dom):
        return pltpu.make_async_remote_copy(
            src_ref=src, dst_ref=dst, send_sem=send, recv_sem=recv,
            device_id=(band, dom), device_id_type=MESH,
        )

    wide = []
    for side in (-1, 1, 0):
        row = lax.rem(h + side + HN, HN)
        for k in range(XN):
            if side != 0 or k != 0:
                wide.append((side, row, columns[k]))
    barrier = pltpu.get_barrier_semaphore()

    def greet(band, dom):
        pl.semaphore_signal(barrier, inc=1, device_id=(band, dom), device_id_type=MESH)

    for side, row, column in wide:
        greet(b, row * XN + column)
    for k in range(XN):
        greet(twin, h * XN + columns[k])
    for band in (up, down, across):
        greet(band, d)
    pl.semaphore_wait(barrier, 18)

    started = []

    def begin(copy):
        copy.start()
        started.append(copy)

    def planes(side, slot_x):
        return pl.ds(pl.multiple_of(((1 - side) * XN + slot_x) * TILE, TILE), TILE)

    mine = pl.ds(4 * c, 4)

    def met(side, column):
        if side == 1:
            return column != 0
        return column != XN - 1

    guarded = []
    for n, (side, row, column) in enumerate(wide):
        copy = remote(
            potential.at[mine], pot.at[mine, planes(side, x), :],
            send_p.at[n], recv_p.at[(1 - side) * XN + x], b, row * XN + column,
        )
        if side == 0:
            begin(copy)
        else:
            sent = met(side, x)
            pl.when(sent)(copy.start)
            guarded.append((sent, copy))
    for n, (side, row, column) in enumerate(wide):
        if side == 0 or n % XN != 2:
            begin(
                remote(
                    window.at[column], even.at[:, planes(side, x), :],
                    send_w.at[n], recv_w.at[(1 - side) * XN + x], b, row * XN + column,
                )
            )
    own = [
        pltpu.make_async_copy(window.at[x], even.at[:, planes(0, x), :], local.at[1]),
        pltpu.make_async_copy(potential.at[mine], pot.at[mine, planes(0, x), :], local.at[2]),
    ]
    for copy in own:
        copy.start()
    keep = pltpu.make_async_copy(states.at[:, mine], rows.at[c], local.at[0])
    keep.start()
    swap = remote(states.at[:, pl.ds(4 * (1 - c), 4)], rows.at[c], send_s, recv_s, twin, d)
    begin(swap)

    flat_rows = rows.reshape(2 * 128 * 32, NY)

    def split_states(core):
        def body(turn, carry):
            for n in range(4):
                k = 4 * turn + n
                value = flat_rows[pl.ds(core * 4096 + k, 128, stride=32), :].T
                upper = value.astype(jnp.bfloat16)
                cells = pl.ds(pl.multiple_of(k * NY, NY), NY)
                lanes = pl.ds(pl.multiple_of(core * 128, 128), 128)
                high[cells, lanes] = upper
                low[cells, lanes] = (value - upper.astype(jnp.float32)).astype(jnp.bfloat16)
            return carry

        lax.fori_loop(0, 8, body, 0)

    keep.wait()
    split_states(c)
    distant = columns[2]
    tile = even.at[:, planes(0, distant), :]
    remote(window.at[0], tile, send_w.at[0], recv_w.at[XN + distant], b, d).wait_recv()
    passed = []
    for n, side in ((2, -1), (6, 1)):
        copy = remote(
            tile, even.at[:, planes(side, distant), :],
            send_w.at[n], recv_w.at[(1 - side) * XN + distant],
            b, lax.rem(h + side + HN, HN) * XN + x,
        )
        copy.start()
        passed.append(copy)
    swap.wait_recv()
    split_states(1 - c)

    own[1].wait()
    for n, side in enumerate((-1, 1, 0)):
        for place, row, column in wide:
            if place != side:
                continue
            copy = remote(
                potential.at[mine], pot.at[mine, planes(side, column), :],
                send_p.at[0], recv_p.at[(1 - side) * XN + column], b, d,
            )
            if side == 0:
                copy.wait_recv()
            else:
                pl.when(met(side, column))(copy.wait_recv)
        low_row, high_row = {1: (8, 32), 0: (32, 64), -1: (64, 88)}[side]
        strip = pot.at[mine, pl.ds(low_row, high_row - low_row), :]
        begin(remote(strip, strip, send_t.at[n], recv_t.at[n], twin, d))

    own[0].wait()
    for n, (side, row, column) in enumerate(wide):
        if side == 0 and n == 9:
            continue
        remote(
            window.at[0], even.at[:, planes(side, column), :],
            send_w.at[0], recv_w.at[(1 - side) * XN + column], b, d,
        ).wait_recv()

    for z in range(NZ):
        product, value = apply_h(even, None, z, 8, 88)
        odd[z, 8:88, :] = (product - CENTRE * value) * (1.0 / HALF_WIDTH)
    for n, side in enumerate((-1, 1, 0)):
        low_row, high_row = {1: (8, 32), 0: (32, 64), -1: (64, 88)}[side]
        strip = pot.at[pl.ds(4 * (1 - c), 4), pl.ds(low_row, high_row - low_row), :]
        remote(strip, strip, send_t.at[n], recv_t.at[n], twin, d).wait_recv()
    for z in range(NZ):
        odd[z, 8:88, :] += pot[z, 8:88, :] * even[z, 8:88, :] * (1.0 / HALF_WIDTH)
    for copy in passed:
        copy.wait_send()
    for source, target, first, last in ((odd, even, 8, 88), (even, odd, 16, 80), (odd, even, 24, 72)):
        for z in range(NZ):
            product, value = apply_h(source, pot, z, first, last)
            target[z, first:last, :] = (
                (product - CENTRE * value) * (2.0 / HALF_WIDTH) - target[z, first:last, :]
            )

    own_pieces = []

    def hand_on(kind, source, offset):
        for k in (0, 1, 3, 2):
            for j in range(2):
                core = lax.rem(c + j, 2)
                place = pl.ds(pl.multiple_of(offset + TILE * columns[k], TILE), TILE)
                piece = source.at[pl.ds(4 * core, 4), place, :]
                goal = gathered.at[q, kind, x, c]
                if k == 0 and j == 0:
                    copy = pltpu.make_async_copy(piece, goal, local.at[3 + kind])
                    copy.start()
                    own_pieces.append(copy)
                else:
                    begin(
                        remote(
                            piece, goal, send_b.at[kind, k, j], recv_b.at[kind, x, c],
                            band_of(q, core), h * XN + columns[k],
                        )
                    )

    hand_on(0, even, 32)
    for z in range(NZ):
        product, value = apply_h(even, pot, z, 32, 64)
        image[z] = product
    hand_on(1, image, 0)

    def forward(chip, kind, k, sems, band):
        place = gathered.at[chip, kind, columns[k]]
        begin(
            remote(place, place, sems.at[chip, kind, k], recv_g.at[chip, kind, k], band, d)
        )

    def arrive(chip, kind, k):
        place = gathered.at[chip, kind, columns[k]]
        remote(
            place, place, send_z.at[chip, kind, k], recv_g.at[chip, kind, k], across, d
        ).wait_recv()

    order = ((0, 0), (0, 1), (0, 3), (1, 0), (0, 2), (1, 1), (1, 3), (1, 2))
    for kind, k in order:
        for j in range(2):
            if k == 0 and j == 0:
                own_pieces[kind].wait()
                continue
            core = lax.rem(c + j, 2)
            remote(
                image.at[pl.ds(0, 4), pl.ds(0, TILE), :], gathered.at[q, kind, columns[k], core],
                send_b.at[0, 0, 0], recv_b.at[kind, columns[k], core], b, d,
            ).wait_recv()
        if kind == 0:
            forward(q, 0, k, send_z, across)
        forward(q, kind, k, send_up, up)
        forward(q, kind, k, send_down, down)
        if kind == 1:
            forward(q, 1, k, send_z, across)

    other = chip_at(1 - zl, 0)
    for k in (0, 1, 3, 2):
        arrive(other, 0, k)
        forward(other, 0, k, send_up, up)
        forward(other, 0, k, send_down, down)

    flat_pieces = gathered.reshape(16 * 512, NY)

    def multiply(chips, last=False):
        count = 16 * len(chips)
        for n, chip in enumerate(chips):
            for k in range(32):
                lanes = slice(NY * k, NY * (k + 1))
                value = flat_pieces[pl.ds(chip * 512 + k, 16, stride=32), :]
                upper = value.astype(jnp.bfloat16)
                left[16 * n : 16 * n + 16, lanes] = upper
                left[count + 16 * n : count + 16 * n + 16, lanes] = (
                    value - upper.astype(jnp.float32)
                ).astype(jnp.bfloat16)
        both = jnp.dot(left[0 : 2 * count, :], high[...], preferred_element_type=jnp.float32)
        rest = jnp.dot(left[0:count, :], low[...], preferred_element_type=jnp.float32)
        product = both[0:count] + (both[count:] + rest)
        for n, chip in enumerate(chips):
            partial[chip] = product[16 * n : 16 * n + 16]
            if last:
                continue
            for core in range(2):
                copy = remote(
                    partial.at[chip, :, pl.ds(128 * core, 128)], parts.at[d * 2 + c],
                    send_r.at[chip, core], recv_r.at[d * 2 + c], band_of(q, core), chip,
                )
                away = jnp.logical_or(chip != d, c != core)
                pl.when(away)(copy.start)
                guarded.append((away, copy))

    def reduce_own():
        def take(source, total):
            remote(
                partial.at[0, :, pl.ds(0, 128)], parts.at[source],
                send_r.at[0, 0], recv_r.at[source], b, d,
            ).wait_recv()
            return total + parts[source]

        total = partial[d, :, pl.ds(pl.multiple_of(128 * c, 128), 128)]
        total = lax.fori_loop(
            0, 16, lambda k, t: take(lax.rem(d + k, 16) * 2 + (1 - c), t), total
        )
        total = lax.fori_loop(1, 16, lambda k, t: take(lax.rem(d + k, 16) * 2 + c, t), total)
        whole[d] = total
        for k in range(1, 16):
            remote(
                whole.at[d], whole.at[d], send_o.at[k], recv_o.at[d], b, lax.rem(d + k, 16)
            ).start()

    ahead = lax.rem(lax.rem(d, YN) - y + YN, YN)
    final = chip_at(1 - zl, 4)
    facing = chip_at(zl, 4)
    apart = jnp.minimum(ahead, YN - ahead)
    turn = jnp.where(lax.div(d, YN) == zl, jnp.maximum(apart, 1), jnp.minimum(apart + 1, 2))
    turn = jnp.where(apart == 3, 3, jnp.where(apart == 4, 5, turn))
    images = ((zl, 1),)
    filtered = ((zl, 0), (1 - zl, 0))

    def ring_step(step, kinds):
        for lo, kind, k in [(lo, kind, k) for lo, kind in kinds for k in (0, 1, 3, 2)]:
            for direction in (1, -1):
                keeps = (k < 2) == (direction == 1)
                if step == 4 and not keeps:
                    continue
                chip = chip_at(lo, -direction * step)
                arrive(chip, kind, k)
                if step < 3 or (step == 3 and keeps):
                    if direction == 1:
                        forward(chip, kind, k, send_up, up)
                    else:
                        forward(chip, kind, k, send_down, down)
                if kind == 1:
                    forward(chip, kind, k, send_z, across)

    def cross(offset):
        for k in (0, 1, 3, 2):
            arrive(chip_at(1 - zl, offset), 1, k)

    def pair(lo, offset):
        return [chip_at(lo, offset), chip_at(lo, -offset)]

    for step in range(1, 4):
        ring_step(step, images)
        if step > 1:
            cross(step - 1)
            cross(1 - step)
            multiply(pair(1 - zl, step - 1))
        ring_step(step, filtered)
        if step == 1:
            cross(0)
            multiply([q, other] + pair(zl, 1))
            continue
        if step == 3:
            ring_step(4, images)
        multiply(pair(zl, step))
        pl.when(turn == step - 1)(reduce_own)

    def near_start(n, chip):
        for k in (2, 1, 3, 0):
            for j in range(2):
                core = lax.rem(c + j, 2)
                part = partial.at[chip, :, pl.ds(pl.multiple_of(128 * core, 128), 128)]
                if k == 0 and j == 0:
                    near[n, x, c] = part[...]
                else:
                    begin(
                        remote(
                            part, near.at[n, x, c], send_near.at[n, k, j], recv_near.at[n, x, c],
                            band_of(q, core), h * XN + columns[k],
                        )
                    )

    def near_finish(n):
        for k in range(XN):
            for j in range(2):
                if k != 0 or j != 0:
                    core = lax.rem(c + j, 2)
                    remote(
                        near.at[n, x, c], near.at[n, columns[k], core], send_near.at[n, 0, 1],
                        recv_near.at[n, columns[k], core], b, d,
                    ).wait_recv()
        total = near[n, 0, 0] + near[n, 0, 1]
        for column in range(1, XN):
            total = total + (near[n, column, 0] + near[n, column, 1])
        far[n, h] = total
        for k in (2, 1, 3):
            begin(
                remote(
                    far.at[n, h], far.at[n, h], send_far.at[n, k], recv_far.at[n, h],
                    b, lax.rem(h + k, HN) * XN + x,
                )
            )

    cross(3)
    cross(-3)
    multiply(pair(1 - zl, 3))
    ring_step(4, filtered)
    cross(4)
    multiply([facing, final], last=True)
    near_start(0, facing)
    near_start(1, final)
    pl.when(turn == 3)(reduce_own)
    near_finish(0)
    near_finish(1)
    for k in range(1, 16):
        source = lax.rem(d + k, 16)
        copy = remote(whole.at[source], whole.at[source], send_o.at[k], recv_o.at[source], b, d)
        pl.when(jnp.logical_and(source != final, source != facing))(copy.wait_recv)
    for n, chip in ((0, facing), (1, final)):
        for k in range(1, HN):
            row = lax.rem(h + k, HN)
            remote(
                far.at[n, h], far.at[n, row], send_far.at[n, k], recv_far.at[n, row], b, d
            ).wait_recv()
        whole[chip] = (far[n, 0] + far[n, 1]) + (far[n, 2] + far[n, 3])
    out[...] = whole[...]

    for copy in started:
        copy.wait_send()
    for sent, copy in guarded:
        pl.when(sent)(copy.wait_send)
    for k in range(1, 16):
        copy = remote(whole.at[d], whole.at[d], send_o.at[k], recv_o.at[d], b, lax.rem(d + k, 16))
        pl.when(turn < 5)(copy.wait_send)


def finish(whole, out_f, out_h, turned):
    flat = whole.reshape(256, 128)
    for kind, out in ((0, out_f), (1, out_h)):
        for column in range(XN):
            for core in range(2):
                turned[pl.ds(4 * core + column, 16, stride=8), :] = flat[
                    pl.ds(8 * kind + 2 * column + core, 16, stride=16), :
                ]
        out[...] = turned[...].T


def per_device(states, window, potential):
    f32 = jnp.float32
    dma = pltpu.SemaphoreType.DMA
    vmem = pltpu.VMEM
    whole = pl.pallas_call(
        kernel,
        out_shape=jax.ShapeDtypeStruct((16, 16, 128), f32),
        in_specs=[pl.BlockSpec(memory_space=pl.ANY)] * 3,
        out_specs=pl.BlockSpec(memory_space=pltpu.VMEM),
        scratch_shapes=[
            vmem((NZ, SPAN, NY), f32),
            vmem((NZ, SPAN, NY), f32),
            vmem((NZ, SPAN, NY), f32),
            vmem((NZ, 32, NY), f32),
            vmem((2, 128, 4, TILE, NY), f32),
            vmem((CELLS, 256), jnp.bfloat16),
            vmem((CELLS, 256), jnp.bfloat16),
            vmem((16, 2, XN, 2, 4, TILE, NY), f32),
            vmem((192, CELLS), jnp.bfloat16),
            vmem((16, 16, 256), f32),
            vmem((32, 16, 128), f32),
            vmem((16, 16, 128), f32),
            vmem((2, XN, 2, 16, 128), f32),
            vmem((2, HN, 16, 128), f32),
            dma((12,)), dma((12,)), dma((12,)), dma((12,)), dma((3,)), dma((3,)),
            dma((5,)), dma, dma,
            dma((2, XN, 2)), dma((2, XN, 2)),
            dma((16, 2, XN)), dma((16, 2, XN)), dma((16, 2, XN)), dma((16, 2, XN)),
            dma((16, 2)), dma((32,)), dma((16,)), dma((16,)),
            dma((2, XN, 2)), dma((2, XN, 2)), dma((2, HN)), dma((2, HN)),
        ],
        compiler_params=pltpu.CompilerParams(
            collective_id=0, has_side_effects=True, vmem_limit_bytes=60 * 1024 * 1024
        ),
    )(states, window, potential)
    return pl.pallas_call(
        finish,
        out_shape=(
            jax.ShapeDtypeStruct((128, 128), f32),
            jax.ShapeDtypeStruct((128, 128), f32),
        ),
        in_specs=[pl.BlockSpec(memory_space=pltpu.VMEM)],
        out_specs=(pl.BlockSpec(memory_space=pltpu.VMEM),) * 2,
        scratch_shapes=[vmem((128, 128), f32)],
    )(whole)


def solution(mesh):
    in_specs = (P("band", None, "dom", None), P("band", None, "dom", None), P(None, "dom", None))
    out_specs = (P("band", None), P("band", None))
    return jax.shard_map(
        per_device, mesh=mesh, in_specs=in_specs, out_specs=out_specs, check_vma=False
    )
```
